32 devices in a mesh: groups: 2 (over y), path: 4 (over z), half: 2 (over x), tile: 2 (over core).
Axes of the slice: x: 2, y: 2, z: 4, core: 2. Of those that a mesh axis runs over, the one named last changes fastest.
Arguments:
- left_prefix: bfloat16 [64, 4096], P(('groups', 'path'), ('half', 'tile')), parts along dimension 0, may hold values from -6 to 6
- right_prefix: bfloat16 [64, 4096], P(('groups', 'half', 'tile'), 'path'), parts along dimension 0, may hold values from -6 to 6
- left_layer: bfloat16 [2048, 1024], P(('groups', 'half', 'tile')), parts along dimension 0, may hold values from -0.1875 to 0.1875
- right_layer: bfloat16 [2048, 1024], P(('groups', 'path')), parts along dimension 0, may hold values from -0.1875 to 0.1875
- left_map: int32 [512], P('groups'), parts along dimension 0, may hold values from 0 to 31
- right_map: int32 [512], P('groups'), parts along dimension 0, may hold values from 0 to 31
- branch_bits: int32 [512, 10], P('groups'), parts along dimension 0, may hold values 0 or 1
- cut_side: int32 [20], P('groups'), parts along dimension 0, may hold values 0 or 1
Outputs:
- amplitude: bfloat16 [8192, 4096], P(('groups', 'half', 'tile'), 'path'), parts along dimension 0
The draws below stay inside these ranges and needn't reach their ends.
There are 2 independent parts, one for each index of `groups`. The reference program is written for one: setup_inputs(seed, part) draws one part's arguments, and reference() takes and returns one part's arrays. A program takes and returns all parts, laid end to end along the dimension named above; each array names one. Nothing has to cross between parts.
All inputs are finite; a program needn't handle non-finite values.
Results may differ from the reference program's by a relative error of at most 0.0058.
Values may be sent and summed in bfloat16 or wider, within the bound.
A program may use at most 64 MiB of HBM per device.

```python
import jax
import jax.numpy as jnp
from jax import lax

CUTS = 10
GATE = 1024
OUT = 4096
PATHS = 256
PREFIX = 32


def with_ends(drawn, rng, low, high):
    place = [jax.random.randint(jax.random.fold_in(rng, axis), (), 0, length) for axis, length in enumerate(drawn.shape)]
    widest = drawn.shape.index(max(drawn.shape))
    neighbour = place[:widest] + [(place[widest] + 1) % drawn.shape[widest]] + place[widest + 1:]
    return drawn.at[tuple(place)].set(low).at[tuple(neighbour)].set(high)


def level_of(key, extent, split, smallest, high):
    factor_of = 1.0
    for dim, shards_of in split:
        draws = jax.random.uniform(jax.random.fold_in(jax.random.fold_in(key, 6), dim), (shards_of,), jnp.float32, smallest / len(split), high / len(split))
        factor_of = factor_of * jnp.repeat(jnp.exp(draws), extent[dim] // shards_of).reshape((-1,) + (1,) * (len(extent) - 1 - dim))
    return factor_of


def centred(key, dims, deviation, reach, split=(), held_as=jnp.bfloat16):
    drawn = deviation * jax.random.normal(key, dims, jnp.float32)
    if split:
        drawn = drawn * level_of(key, dims, split, -0.22, 0.18)
    return jnp.clip(drawn, -reach, reach).astype(held_as)


def setup_inputs(seed: int = 0, part: int = 0) -> dict:
    key_of = jax.random.split(jax.random.key(seed), 9)
    own_keys = jax.random.split(jax.random.fold_in(key_of[8], part), 9)
    return {
        "left_prefix": centred(own_keys[0], (PREFIX, OUT), 1.0, 6.0, ((0, 4), (1, 4))),
        "right_prefix": centred(own_keys[1], (PREFIX, OUT), 1.0, 6.0, ((0, 4), (1, 4))),
        "left_layer": centred(own_keys[2], (GATE, GATE), GATE ** -0.5, 0.1875, ((0, 4),)),
        "right_layer": centred(own_keys[3], (GATE, GATE), GATE ** -0.5, 0.1875, ((0, 4),)),
        "left_map": with_ends(jax.random.randint(own_keys[4], (PATHS,), 0, PREFIX), jax.random.fold_in(own_keys[4], 1), 0, PREFIX - 1).astype(jnp.int32),
        "right_map": with_ends(jax.random.randint(own_keys[5], (PATHS,), 0, PREFIX), jax.random.fold_in(own_keys[5], 1), 0, PREFIX - 1).astype(jnp.int32),
        "branch_bits": with_ends((jax.random.randint(own_keys[6], (PATHS, CUTS), 0, 2) < 1).astype(jnp.int32), jax.random.fold_in(own_keys[6], 1), 0, 1),
        "cut_side": with_ends((jax.random.randint(own_keys[7], (CUTS,), 0, 2) < 1).astype(jnp.int32), jax.random.fold_in(own_keys[7], 1), 0, 1),
    }


def cut_factors(branch, cut_side, gate_count, on_left):
    cut_count = cut_side.shape[0]
    bit_place = lax.broadcasted_iota(jnp.int32, (cut_count, gate_count), 0)
    gate_code = lax.broadcasted_iota(jnp.int32, (cut_count, gate_count), 1)
    bit_table = jnp.right_shift(gate_code, bit_place) & 1
    projector = cut_side if on_left else 1 - cut_side
    phased = 1 - projector
    chosen = branch * projector[None, :]
    misses = jnp.sum(chosen, axis=1, keepdims=True) + jnp.dot(projector, bit_table)[None, :] - 2 * jnp.dot(chosen, bit_table)
    parity = jnp.dot(branch * phased[None, :], bit_table)
    sign_value = 1 - 2 * (parity % 2)
    return jnp.where(misses == 0, sign_value, 0).astype(jnp.float32)


def half_states(prefix, path_map, branch, cut_side, layer_matrix, on_left):
    gate_count = layer_matrix.shape[0]
    blocks = prefix.shape[1] // gate_count
    count = path_map.shape[0]
    picked = prefix[path_map].reshape(count, blocks, gate_count)
    factor = cut_factors(branch, cut_side, gate_count, on_left)
    projected = (picked.astype(jnp.float32) * factor[:, None, :]).astype(jnp.bfloat16)
    states = jnp.dot(projected.reshape(count * blocks, gate_count), layer_matrix.T, preferred_element_type=jnp.float32)
    return states.astype(jnp.bfloat16).reshape(count, blocks * gate_count)


def reference(left_prefix, right_prefix, left_layer, right_layer, left_map, right_map, branch_bits, cut_side):
    left_states = half_states(left_prefix, left_map, branch_bits, cut_side, left_layer, True)
    right_states = half_states(right_prefix, right_map, branch_bits, cut_side, right_layer, False)
    amplitude = lax.dot_general(left_states, right_states, (((0,), (0,)), ((), ())), preferred_element_type=jnp.float32)
    return amplitude.astype(jnp.bfloat16)
```

```python
import functools

import jax
import jax.numpy as jnp
from jax import lax
from jax.experimental import pallas as pl
from jax.experimental.pallas import tpu as pltpu
from jax.sharding import PartitionSpec as P

MESH = pl.DeviceIdType.MESH
NT = (((1,), (1,)), ((), ()))


def factors(branch, side, gate_count):
    cuts = branch.shape[1]
    place = lax.broadcasted_iota(jnp.int32, (cuts, gate_count), 0)
    code = lax.broadcasted_iota(jnp.int32, (cuts, gate_count), 1)
    bits = (jnp.right_shift(code, place) & 1).astype(jnp.float32).astype(jnp.bfloat16)

    def dot(rows):
        return jnp.dot(rows.astype(jnp.bfloat16), bits, preferred_element_type=jnp.float32)

    made = []
    for projector in (side, 1.0 - side):
        chosen = branch * projector
        misses = jnp.sum(chosen, axis=1, keepdims=True) + dot(projector - 2.0 * chosen)
        parity = dot(branch - chosen).astype(jnp.int32) & 1
        sign = (1 - 2 * parity).astype(jnp.float32)
        made.append(jnp.where(misses == 0.0, sign, 0.0))
    return made


def picked_rows(prefix_ref, path_map):
    shards, rows, gate_count = prefix_ref.shape
    prefix = prefix_ref[...].astype(jnp.float32).reshape(shards * rows, gate_count)
    which = lax.broadcasted_iota(jnp.int32, (shards * rows, path_map.shape[1]), 0)
    hot = jnp.where(which == path_map, 1.0, 0.0).T
    return jnp.dot(
        hot.astype(jnp.bfloat16), prefix.astype(jnp.bfloat16), preferred_element_type=jnp.float32
    )


def kernel(
    sizes,
    left_prefix, right_prefix, left_layer, right_layer, left_map, right_map, branch_bits, cut_side,
    left_out, right_out,
    left_rows, right_rows, left_proj, right_proj, left_w, right_w,
    own_sem, pre_send, pre_recv,
    r_send, r_recv, r_sib_send, r_sib_recv,
    l_send, l_recv, l_sib_send, l_sib_recv, o_send, o_recv,
):
    n_half, n_path, n_tile = sizes
    x, z, c = lax.axis_index("half"), lax.axis_index("path"), lax.axis_index("tile")
    sib = 1 - c
    n_lr = n_half * n_tile
    mine = x * n_tile + c

    barrier = pltpu.get_barrier_semaphore()
    for k in range(1, n_path):
        pl.semaphore_signal(
            barrier, inc=1, device_id={"path": lax.rem(z + k, n_path)}, device_id_type=MESH
        )
    for k in range(1, n_lr):
        there = lax.rem(mine + k, n_lr)
        pl.semaphore_signal(
            barrier,
            inc=1,
            device_id={"half": there // n_tile, "tile": lax.rem(there, n_tile)},
            device_id_type=MESH,
        )

    block_l, gate = left_layer.shape
    block_r = right_layer.shape[0]
    part_r = block_r // n_tile
    chunk_r = max(16, part_r // 2)
    chunk_l = max(16, block_l // 4)
    count_r, count_l = part_r // chunk_r, block_l // chunk_l

    own = [
        pltpu.make_async_copy(left_prefix, left_rows.at[z], own_sem.at[0]),
        pltpu.make_async_copy(right_prefix, right_rows.at[mine], own_sem.at[1]),
        pltpu.make_async_copy(
            left_layer, left_w.at[pl.ds(pl.multiple_of(mine * block_l, block_l), block_l)], own_sem.at[2]
        ),
        pltpu.make_async_copy(
            right_layer, right_w.at[pl.ds(pl.multiple_of(z * block_r, block_r), block_r)], own_sem.at[3]
        ),
    ]
    for copy in own:
        copy.start()

    side = cut_side[...].astype(jnp.float32)
    branch = branch_bits[...].astype(jnp.float32)
    for ref, factor in zip((left_proj, right_proj), factors(branch, side, gate)):
        ref[...] = factor.astype(jnp.bfloat16)

    pl.semaphore_wait(barrier, n_path - 1 + n_lr - 1)

    def remote(src, dst, send, recv, device):
        return pltpu.make_async_remote_copy(
            src_ref=src, dst_ref=dst, send_sem=send, recv_sem=recv, device_id=device, device_id_type=MESH
        )

    prefix_copies = []
    for k in range(1, n_path):
        prefix_copies.append(remote(
            left_prefix, left_rows.at[z], pre_send.at[k - 1], pre_recv.at[k - 1],
            {"path": lax.rem(z + k, n_path)},
        ))
    for k in range(1, n_lr):
        there = lax.rem(mine + k, n_lr)
        slot = n_path - 1 + k - 1
        prefix_copies.append(remote(
            right_prefix, right_rows.at[mine], pre_send.at[slot], pre_recv.at[slot],
            {"half": there // n_tile, "tile": lax.rem(there, n_tile)},
        ))
    for copy in prefix_copies:
        copy.start()

    def rows_r(block, core, i):
        return pl.ds(pl.multiple_of(block * block_r + core * part_r + i * chunk_r, chunk_r), chunk_r)

    def rows_l(block, core, i):
        return pl.ds(
            pl.multiple_of((block * n_tile + core) * block_l + i * chunk_l, chunk_l), chunk_l
        )

    class Line:
        def __init__(self, axis, pos, n, rows, buf, first, out, proj, count, sems):
            self.axis, self.pos, self.n, self.rows, self.buf = axis, pos, n, rows, buf
            self.first, self.out, self.proj, self.count = first, out, proj, count
            self.send, self.recv, self.sib_send, self.sib_recv = sems
            self.slots = (n - 1) * count

        def block(self, way, d):
            return self.pos - d if way == 0 else self.pos + d

        def has(self, way, d):
            return (self.pos >= d) if way == 0 else (self.pos + d < self.n)

        def sends(self, way, d):
            onward = (self.pos + 1 < self.n) if way == 0 else (self.pos >= 1)
            return jnp.logical_and(self.has(way, d), onward)

        def onward(self, way, d, i, own=False):
            span = self.rows(self.block(way, d), c, i)
            src = self.first(i) if own else self.buf.at[span]
            at = d * self.count + i
            return remote(
                src, self.buf.at[span], self.send.at[way, at], self.recv.at[way, at],
                {self.axis: self.pos + (1 if way == 0 else -1)},
            )

        def arrived(self, way, d, i):
            span = self.rows(self.block(way, d), c, i)
            at = (d - 1) * self.count + i
            return remote(
                self.buf.at[span], self.buf.at[span], self.send.at[way, at], self.recv.at[way, at],
                {self.axis: self.pos + (1 if way == 0 else -1)},
            )

        def share(self, way, d, i, core):
            span = self.rows(self.block(way, d), core, i)
            at = (d - 1) * self.count + i
            return remote(
                self.buf.at[span], self.buf.at[span],
                self.sib_send.at[way, at], self.sib_recv.at[way, at], {"tile": sib},
            )

        def start_own(self, i):
            for way in (0, 1):
                @pl.when(self.sends(way, 0))
                def _():
                    self.onward(way, 0, i, own=True).start()

        def relay(self, s):
            d, i = s // self.count + 1, lax.rem(s, self.count)
            for way in (0, 1):
                @pl.when(jnp.logical_and(s < self.slots, self.has(way, d)))
                def _():
                    self.arrived(way, d, i).wait_recv()
                    @pl.when(jnp.logical_and(self.sends(way, d), d < self.n - 1))
                    def _():
                        self.onward(way, d, i).start()
                    self.share(way, d, i, c).start()

        def multiply(self, span):
            self.out[span, :] = lax.dot_general(
                self.buf[span, :], self.proj[...], NT, preferred_element_type=jnp.float32
            ).astype(self.out.dtype)

        def compute(self, s):
            d, i = s // self.count + 1, lax.rem(s, self.count)
            for way in (0, 1):
                @pl.when(jnp.logical_and(s < self.slots, self.has(way, d)))
                def _():
                    self.multiply(self.rows(self.block(way, d), c, i))

        def compute_shared(self, s):
            d, i = s // self.count + 1, lax.rem(s, self.count)
            for way in (0, 1):
                @pl.when(jnp.logical_and(jnp.logical_and(s >= 0, s < self.slots), self.has(way, d)))
                def _():
                    self.share(way, d, i, sib).wait_recv()
                    self.multiply(self.rows(self.block(way, d), sib, i))

        def finish(self, s):
            d, i = s // self.count, lax.rem(s, self.count)
            for way in (0, 1):
                @pl.when(self.sends(way, d))
                def _():
                    self.onward(way, d, i).wait_send()
                @pl.when(self.has(way, d + 1))
                def _():
                    self.share(way, d + 1, i, c).wait_send()

    right = Line(
        "path", z, n_path, rows_r, right_w,
        lambda i: right_layer.at[pl.ds(pl.multiple_of(c * part_r + i * chunk_r, chunk_r), chunk_r)],
        right_out, right_proj, count_r, (r_send, r_recv, r_sib_send, r_sib_recv),
    )
    left = Line(
        "half", x, n_half, rows_l, left_w,
        lambda i: left_layer.at[pl.ds(i * chunk_l, chunk_l)],
        left_out, left_proj, count_l, (l_send, l_recv, l_sib_send, l_sib_recv),
    )

    def own_share(i, core):
        span = rows_l(x, core, i)
        return remote(
            left.first(i), left_w.at[span], o_send.at[i], o_recv.at[i], {"tile": sib}
        )

    for i in range(max(count_r, count_l)):
        if i < count_r:
            right.start_own(i)
        if i < count_l:
            left.start_own(i)
    for i in range(count_l):
        own_share(i, c).start()

    for copy in own:
        copy.wait()
    for copy in prefix_copies:
        copy.wait_recv()
    for ref, rows, path_map in ((left_proj, left_rows, left_map), (right_proj, right_rows, right_map)):
        chosen = picked_rows(rows, path_map[...])
        ref[...] = (chosen * ref[...].astype(jnp.float32)).astype(jnp.bfloat16)

    left.multiply(pl.ds(pl.multiple_of(mine * block_l, block_l), block_l))
    right.multiply(pl.ds(pl.multiple_of(z * block_r, block_r), block_r))

    slots = max(right.slots, left.slots)

    def step(s, _):
        right.relay(s)
        left.relay(s)
        right.compute_shared(s - 1)
        left.compute_shared(s - 1)
        right.compute(s)
        left.compute(s)
        return 0

    def shared_block():
        for i in range(count_l):
            own_share(i, sib).wait_recv()
        left.multiply(pl.ds(pl.multiple_of((x * n_tile + sib) * block_l, block_l), block_l))

    if slots > 0:
        lax.fori_loop(0, 1, step, 0)
    shared_block()
    if slots > 1:
        lax.fori_loop(1, slots, step, 0)
    right.compute_shared(jnp.int32(slots - 1))
    left.compute_shared(jnp.int32(slots - 1))

    for line in (right, left):
        if line.slots > 0:
            lax.fori_loop(0, line.slots, lambda s, _, line=line: (line.finish(s), 0)[1], 0)
    for i in range(count_l):
        own_share(i, c).wait_send()
    for copy in prefix_copies:
        copy.wait_send()


def on_device(
    sizes,
    left_prefix, right_prefix, left_layer, right_layer, left_map, right_map, branch_bits, cut_side,
):
    n_half, n_path, n_tile = sizes
    n_lr = n_half * n_tile
    paths = left_map.shape[0]
    gate = left_layer.shape[1]
    hi_l, hi_r = left_layer.shape[0] * n_lr, right_layer.shape[0] * n_path
    part_r = right_layer.shape[0] // n_tile
    count_r = part_r // max(16, part_r // 2)
    count_l = left_layer.shape[0] // max(16, left_layer.shape[0] // 4)
    slots_r = max(1, (n_path - 1) * count_r)
    slots_l = max(1, (n_half - 1) * count_l)
    pre = n_path + n_lr - 2
    dma = pltpu.SemaphoreType.DMA
    vmem = pl.BlockSpec(memory_space=pltpu.VMEM)
    anywhere = pl.BlockSpec(memory_space=pl.ANY)
    left_states, right_states = pl.pallas_call(
        functools.partial(kernel, sizes),
        out_shape=(
            jax.ShapeDtypeStruct((hi_l, paths), jnp.bfloat16),
            jax.ShapeDtypeStruct((hi_r, paths), jnp.bfloat16),
        ),
        in_specs=[anywhere] * 4 + [vmem] * 4,
        out_specs=(vmem, vmem),
        scratch_shapes=[
            pltpu.VMEM((n_path,) + left_prefix.shape, jnp.bfloat16),
            pltpu.VMEM((n_lr,) + right_prefix.shape, jnp.bfloat16),
            pltpu.VMEM((paths, gate), jnp.bfloat16),
            pltpu.VMEM((paths, gate), jnp.bfloat16),
            pltpu.VMEM((hi_l, gate), jnp.bfloat16),
            pltpu.VMEM((hi_r, gate), jnp.bfloat16),
            dma((4,)), dma((pre,)), dma((pre,)),
            dma((2, slots_r)), dma((2, slots_r)), dma((2, slots_r)), dma((2, slots_r)),
            dma((2, slots_l)), dma((2, slots_l)), dma((2, slots_l)), dma((2, slots_l)),
            dma((count_l,)), dma((count_l,)),
        ],
        compiler_params=pltpu.CompilerParams(collective_id=0, has_side_effects=True),
    )(
        left_prefix, right_prefix, left_layer, right_layer,
        left_map[None, :], right_map[None, :], branch_bits, cut_side[None, :],
    )
    amplitude = lax.dot_general(
        left_states, right_states, NT, preferred_element_type=jnp.float32
    )
    return amplitude.astype(jnp.bfloat16)


def solution(mesh):
    in_specs = (
        P(("groups", "path"), ("half", "tile")),
        P(("groups", "half", "tile"), "path"),
        P(("groups", "half", "tile"), None),
        P(("groups", "path"), None),
        P("groups"),
        P("groups"),
        P("groups", None),
        P("groups"),
    )
    out_specs = P(("groups", "half", "tile"), "path")
    sizes = tuple(mesh.shape[axis] for axis in ("half", "path", "tile"))
    return jax.shard_map(
        functools.partial(on_device, sizes),
        mesh=mesh, in_specs=in_specs, out_specs=out_specs, check_vma=False,
    )
```

```python
import functools

import jax
import jax.numpy as jnp
from jax import lax
from jax.experimental import pallas as pl
from jax.experimental.pallas import tpu as pltpu
from jax.sharding import PartitionSpec as P

MESH = pl.DeviceIdType.MESH
NT = (((1,), (1,)), ((), ()))
TN = (((0,), (0,)), ((), ()))


def factors(branch, side_row, gate_count):
    cuts = branch.shape[0]
    across = lax.broadcasted_iota(jnp.int32, (cuts, cuts), 0)
    down = lax.broadcasted_iota(jnp.int32, (cuts, cuts), 1)
    side = jnp.sum(jnp.where(across == down, side_row, 0.0), axis=1, keepdims=True)
    place = lax.broadcasted_iota(jnp.int32, (cuts, gate_count), 0)
    code = lax.broadcasted_iota(jnp.int32, (cuts, gate_count), 1)
    bits = (jnp.right_shift(code, place) & 1).astype(jnp.float32)

    def dot(columns, table):
        return lax.dot_general(
            columns.astype(jnp.bfloat16), table.astype(jnp.bfloat16), TN,
            preferred_element_type=jnp.float32,
        )

    made = []
    for projector in (side, 1.0 - side):
        chosen = branch * projector
        misses = dot(chosen, 1.0 - bits) + dot(projector - chosen, bits)
        parity = dot(branch - chosen, bits).astype(jnp.int32) & 1
        sign = (1 - 2 * parity).astype(jnp.float32)
        made.append(jnp.where(misses == 0.0, sign, 0.0))
    return made


def picked_rows(prefix, path_map):
    shards, rows, gate_count = prefix.shape
    prefix = prefix.astype(jnp.float32).reshape(shards * rows, gate_count)
    which = lax.broadcasted_iota(jnp.int32, (shards * rows, path_map.shape[1]), 0)
    hot = jnp.where(which == path_map, 1.0, 0.0).T
    return jnp.dot(
        hot.astype(jnp.bfloat16), prefix.astype(jnp.bfloat16), preferred_element_type=jnp.float32
    )


def kernel(
    sizes,
    left_prefix, right_prefix, left_layer, right_layer, left_map, right_map, branch_bits, cut_side,
    left_out, right_out,
    left_rows, right_rows, left_proj, right_factor, right_proj, left_w, right_w,
    left_st, right_st, stage,
    own_sem, pre_send, pre_recv,
    pz_send, pz_recv, ps_send, ps_recv,
    st_send, st_recv, ss_send, ss_recv,
    l_send, l_recv, l_sib_send, l_sib_recv, o_send, o_recv, lo_sem, ro_sem,
):
    n_half, n_path, n_tile = sizes
    x, z, c = lax.axis_index("half"), lax.axis_index("path"), lax.axis_index("tile")
    sib = 1 - c
    n_lr = n_half * n_tile
    mine = x * n_tile + c

    barrier = pltpu.get_barrier_semaphore()
    for k in range(1, n_path):
        pl.semaphore_signal(
            barrier, inc=1, device_id={"path": lax.rem(z + k, n_path)}, device_id_type=MESH
        )
    for k in range(1, n_lr):
        there = lax.rem(mine + k, n_lr)
        pl.semaphore_signal(
            barrier,
            inc=1,
            device_id={"half": there // n_tile, "tile": lax.rem(there, n_tile)},
            device_id_type=MESH,
        )

    block_l, gate = left_layer.shape
    block_r = right_layer.shape[0]
    part_r = block_r // n_tile
    chunk_l = max(16, block_l // 4)
    count_l = block_l // chunk_l
    half_lr = n_lr // n_tile

    own = [
        pltpu.make_async_copy(left_prefix, left_rows.at[z], own_sem.at[0]),
        pltpu.make_async_copy(right_prefix, right_rows.at[z, mine], own_sem.at[1]),
        pltpu.make_async_copy(
            left_layer, left_w.at[pl.ds(pl.multiple_of(mine * block_l, block_l), block_l)], own_sem.at[2]
        ),
        pltpu.make_async_copy(right_layer, right_w, own_sem.at[3]),
    ]
    for copy in own:
        copy.start()

    side = cut_side[...].astype(jnp.float32)
    branch = branch_bits[...].astype(jnp.float32)
    for ref, factor in zip((left_proj, right_factor), factors(branch, side, gate)):
        ref[...] = factor.astype(jnp.bfloat16)

    pl.semaphore_wait(barrier, n_path - 1 + n_lr - 1)

    def remote(src, dst, send, recv, device):
        return pltpu.make_async_remote_copy(
            src_ref=src, dst_ref=dst, send_sem=send, recv_sem=recv, device_id=device, device_id_type=MESH
        )

    prefix_copies = []
    for k in range(1, n_path):
        prefix_copies.append(remote(
            left_prefix, left_rows.at[z], pre_send.at[k - 1], pre_recv.at[k - 1],
            {"path": lax.rem(z + k, n_path)},
        ))
    for k in range(1, n_lr):
        there = lax.rem(mine + k, n_lr)
        slot = n_path - 1 + k - 1
        prefix_copies.append(remote(
            right_prefix, right_rows.at[z, mine], pre_send.at[slot], pre_recv.at[slot],
            {"half": there // n_tile, "tile": lax.rem(there, n_tile)},
        ))
    for copy in prefix_copies:
        copy.start()

    def rows_l(block, core, i):
        return pl.ds(
            pl.multiple_of((block * n_tile + core) * block_l + i * chunk_l, chunk_l), chunk_l
        )

    def left_flush(block, core, i):
        span = rows_l(block, core, i)
        at = (block * n_tile + core) * count_l + i
        return pltpu.make_async_copy(left_st.at[span], left_out.at[span], lo_sem.at[at])

    def part(block, core):
        return pl.ds(pl.multiple_of(block * block_r + core * part_r, part_r), part_r)

    def right_flush(block, core):
        span = part(block, core)
        return pltpu.make_async_copy(
            right_st.at[span], right_out.at[span], ro_sem.at[block * n_tile + core]
        )

    class Line:
        def __init__(self, axis, pos, n, rows, buf, first, proj, count, sems):
            self.axis, self.pos, self.n, self.rows, self.buf = axis, pos, n, rows, buf
            self.first, self.proj, self.count = first, proj, count
            self.send, self.recv, self.sib_send, self.sib_recv = sems
            self.slots = (n - 1) * count

        def block(self, way, d):
            return self.pos - d if way == 0 else self.pos + d

        def has(self, way, d):
            return (self.pos >= d) if way == 0 else (self.pos + d < self.n)

        def sends(self, way, d):
            onward = (self.pos + 1 < self.n) if way == 0 else (self.pos >= 1)
            return jnp.logical_and(self.has(way, d), onward)

        def onward(self, way, d, i, own=False):
            span = self.rows(self.block(way, d), c, i)
            src = self.first(i) if own else self.buf.at[span]
            at = d * self.count + i
            return remote(
                src, self.buf.at[span], self.send.at[way, at], self.recv.at[way, at],
                {self.axis: self.pos + (1 if way == 0 else -1)},
            )

        def arrived(self, way, d, i):
            span = self.rows(self.block(way, d), c, i)
            at = (d - 1) * self.count + i
            return remote(
                self.buf.at[span], self.buf.at[span], self.send.at[way, at], self.recv.at[way, at],
                {self.axis: self.pos + (1 if way == 0 else -1)},
            )

        def share(self, way, d, i, core):
            span = self.rows(self.block(way, d), core, i)
            at = (d - 1) * self.count + i
            return remote(
                self.buf.at[span], self.buf.at[span],
                self.sib_send.at[way, at], self.sib_recv.at[way, at], {"tile": sib},
            )

        def start_own(self, i):
            for way in (0, 1):
                @pl.when(self.sends(way, 0))
                def _():
                    self.onward(way, 0, i, own=True).start()

        def relay(self, s):
            d, i = s // self.count + 1, lax.rem(s, self.count)
            for way in (0, 1):
                @pl.when(jnp.logical_and(s < self.slots, self.has(way, d)))
                def _():
                    self.arrived(way, d, i).wait_recv()
                    @pl.when(jnp.logical_and(self.sends(way, d), d < self.n - 1))
                    def _():
                        self.onward(way, d, i).start()
                    self.share(way, d, i, c).start()

        def multiply(self, block, core, i):
            span = self.rows(block, core, i)
            left_st[span, :] = lax.dot_general(
                self.buf[span, :], self.proj[...], NT, preferred_element_type=jnp.float32
            ).astype(jnp.bfloat16)
            left_flush(block, core, i).start()

        def compute(self, s):
            d, i = s // self.count + 1, lax.rem(s, self.count)
            for way in (0, 1):
                @pl.when(jnp.logical_and(s < self.slots, self.has(way, d)))
                def _():
                    self.multiply(self.block(way, d), c, i)

        def compute_shared(self, s):
            d, i = s // self.count + 1, lax.rem(s, self.count)
            for way in (0, 1):
                @pl.when(jnp.logical_and(jnp.logical_and(s >= 0, s < self.slots), self.has(way, d)))
                def _():
                    self.share(way, d, i, sib).wait_recv()
                    self.multiply(self.block(way, d), sib, i)

        def finish(self, s):
            d, i = s // self.count, lax.rem(s, self.count)
            for way in (0, 1):
                @pl.when(self.sends(way, d))
                def _():
                    self.onward(way, d, i).wait_send()
                @pl.when(self.has(way, d + 1))
                def _():
                    self.share(way, d + 1, i, c).wait_send()

    left = Line(
        "half", x, n_half, rows_l, left_w,
        lambda i: left_layer.at[pl.ds(i * chunk_l, chunk_l)],
        left_proj, count_l, (l_send, l_recv, l_sib_send, l_sib_recv),
    )

    def own_share(i, core):
        span = rows_l(x, core, i)
        return remote(
            left.first(i), left_w.at[span], o_send.at[i], o_recv.at[i], {"tile": sib}
        )

    for i in range(count_l):
        left.start_own(i)
    for i in range(count_l):
        own_share(i, c).start()

    def prefix_half(block, core):
        return right_rows.at[block, pl.ds(core * half_lr, half_lr)]

    def prefix_out(to):
        held = prefix_half(z, c)
        return remote(held, held, pz_send.at[to], pz_recv.at[z], {"path": to})

    def prefix_in(block):
        held = prefix_half(block, c)
        return remote(held, held, pz_send.at[block], pz_recv.at[block], {"path": block})

    def prefix_share(block, core):
        held = prefix_half(block, core)
        return remote(held, held, ps_send.at[block], ps_recv.at[block], {"tile": sib})

    def state_out(to):
        return remote(
            stage.at[to], right_st.at[part(z, c)], st_send.at[to], st_recv.at[z], {"path": to}
        )

    def state_in(block):
        return remote(
            stage.at[block], right_st.at[part(block, c)], st_send.at[block], st_recv.at[block],
            {"path": block},
        )

    def state_share(block, core):
        held = right_st.at[part(block, core)]
        return remote(held, held, ss_send.at[block], ss_recv.at[block], {"tile": sib})

    def each(d, do):
        @pl.when(z >= d)
        def _():
            do(z - d)
        @pl.when(z + d < n_path)
        def _():
            do(z + d)

    own[1].wait()
    for copy in prefix_copies[n_path - 1:]:
        copy.wait_recv()
    def far_first(k, _):
        each(n_path - 1 - k, lambda to: prefix_out(to).start())
        return 0
    if n_path > 1:
        lax.fori_loop(0, n_path - 1, far_first, 0)

    def project_right(block):
        chosen = picked_rows(right_rows[block], right_map[...])
        right_proj[...] = (chosen * right_factor[...].astype(jnp.float32)).astype(jnp.bfloat16)

    def right_times(rows):
        return lax.dot_general(
            rows, right_proj[...], NT, preferred_element_type=jnp.float32
        ).astype(jnp.bfloat16)

    own[0].wait()
    for copy in prefix_copies[:n_path - 1]:
        copy.wait_recv()
    chosen = picked_rows(left_rows[...], left_map[...])
    left_proj[...] = (chosen * left_proj[...].astype(jnp.float32)).astype(jnp.bfloat16)
    own[2].wait()
    own[3].wait()

    def right_step(d):
        def pass_on(block):
            prefix_in(block).wait_recv()
            prefix_share(block, c).start()
        each(d, pass_on)

        def form(block):
            prefix_share(block, sib).wait_recv()
            project_right(block)
            stage[block] = right_times(right_w[pl.ds(pl.multiple_of(c * part_r, part_r), part_r), :])
            state_out(block).start()
        each(d, form)

    def left_step(s):
        left.relay(s)
        left.compute_shared(s - 1)
        left.compute(s)

    project_right(z)
    for core in range(n_tile):
        right_st[part(z, core), :] = right_times(right_w[core * part_r:(core + 1) * part_r, :])
        right_flush(z, core).start()
    for i in range(count_l):
        left.multiply(x, c, i)

    steps = max(n_path - 1, left.slots)

    def step(t, _):
        @pl.when(t < n_path - 1)
        def _():
            right_step(t + 1)
        left_step(t)
        return 0

    def shared_block():
        for i in range(count_l):
            own_share(i, sib).wait_recv()
            left.multiply(x, sib, i)

    shared_block()
    both = min(n_path - 1, left.slots)
    if both > 0:
        lax.fori_loop(0, both, step, 0)
    if n_path - 1 > both:
        lax.fori_loop(both, n_path - 1, lambda t, _: (right_step(t + 1), 0)[1], 0)

    def take(k, _):
        def landed(block):
            state_in(block).wait_recv()
            state_share(block, c).start()
            right_flush(block, c).start()
        each(k + 1, landed)
        return 0

    if n_path > 1:
        lax.fori_loop(0, n_path - 1, take, 0)
    if left.slots > both:
        lax.fori_loop(both, left.slots, lambda t, _: (left_step(t), 0)[1], 0)

    def take_shared(k, _):
        def landed(block):
            state_share(block, sib).wait_recv()
            right_flush(block, sib).start()
        each(k + 1, landed)
        return 0

    if n_path > 1:
        lax.fori_loop(0, n_path - 1, take_shared, 0)
    left.compute_shared(jnp.int32(left.slots - 1))

    def close(k, _):
        def ended(block):
            prefix_out(block).wait_send()
            prefix_share(block, c).wait_send()
            state_out(block).wait_send()
            state_share(block, c).wait_send()
        each(k + 1, ended)
        return 0

    if n_path > 1:
        lax.fori_loop(0, n_path - 1, close, 0)
    if left.slots > 0:
        lax.fori_loop(0, left.slots, lambda s, _: (left.finish(s), 0)[1], 0)
    for i in range(count_l):
        own_share(i, c).wait_send()
    for copy in prefix_copies:
        copy.wait_send()

    def flushed_left(k, _):
        for core in range(n_tile):
            for i in range(count_l):
                left_flush(k, core, i).wait()
        return 0

    def flushed_right(k, _):
        for core in range(n_tile):
            right_flush(k, core).wait()
        return 0

    lax.fori_loop(0, n_half, flushed_left, 0)
    lax.fori_loop(0, n_path, flushed_right, 0)


def on_device(
    sizes,
    left_prefix, right_prefix, left_layer, right_layer, left_map, right_map, branch_bits, cut_side,
):
    n_half, n_path, n_tile = sizes
    n_lr = n_half * n_tile
    paths = left_map.shape[0]
    gate = left_layer.shape[1]
    hi_l, hi_r = left_layer.shape[0] * n_lr, right_layer.shape[0] * n_path
    part_r = right_layer.shape[0] // n_tile
    count_l = left_layer.shape[0] // max(16, left_layer.shape[0] // 4)
    slots_l = max(1, (n_half - 1) * count_l)
    pre = n_path + n_lr - 2
    dma = pltpu.SemaphoreType.DMA
    vmem = pl.BlockSpec(memory_space=pltpu.VMEM)
    anywhere = pl.BlockSpec(memory_space=pl.ANY)
    left_states, right_states = pl.pallas_call(
        functools.partial(kernel, sizes),
        out_shape=(
            jax.ShapeDtypeStruct((hi_l, paths), jnp.bfloat16),
            jax.ShapeDtypeStruct((hi_r, paths), jnp.bfloat16),
        ),
        in_specs=[anywhere] * 4 + [vmem] * 4,
        out_specs=(anywhere, anywhere),
        scratch_shapes=[
            pltpu.VMEM((n_path,) + left_prefix.shape, jnp.bfloat16),
            pltpu.VMEM((n_path, n_lr) + right_prefix.shape, jnp.bfloat16),
            pltpu.VMEM((paths, gate), jnp.bfloat16),
            pltpu.VMEM((paths, gate), jnp.bfloat16),
            pltpu.VMEM((paths, gate), jnp.bfloat16),
            pltpu.VMEM((hi_l, gate), jnp.bfloat16),
            pltpu.VMEM(right_layer.shape, jnp.bfloat16),
            pltpu.VMEM((hi_l, paths), jnp.bfloat16),
            pltpu.VMEM((hi_r, paths), jnp.bfloat16),
            pltpu.VMEM((n_path, part_r, paths), jnp.bfloat16),
            dma((4,)), dma((pre,)), dma((pre,)),
        ] + [dma((n_path,))] * 8 + [
            dma((2, slots_l)), dma((2, slots_l)), dma((2, slots_l)), dma((2, slots_l)),
            dma((count_l,)), dma((count_l,)),
            dma((n_lr * count_l,)), dma((n_path * n_tile,)),
        ],
        compiler_params=pltpu.CompilerParams(collective_id=0, has_side_effects=True),
    )(
        left_prefix, right_prefix, left_layer, right_layer,
        left_map[None, :], right_map[None, :], branch_bits.T, cut_side[None, :],
    )
    amplitude = lax.dot_general(
        left_states, right_states, NT, preferred_element_type=jnp.float32
    )
    return amplitude.astype(jnp.bfloat16)


def solution(mesh):
    in_specs = (
        P(("groups", "path"), ("half", "tile")),
        P(("groups", "half", "tile"), "path"),
        P(("groups", "half", "tile"), None),
        P(("groups", "path"), None),
        P("groups"),
        P("groups"),
        P("groups", None),
        P("groups"),
    )
    out_specs = P(("groups", "half", "tile"), "path")
    sizes = tuple(mesh.shape[axis] for axis in ("half", "path", "tile"))
    return jax.shard_map(
        functools.partial(on_device, sizes),
        mesh=mesh, in_specs=in_specs, out_specs=out_specs, check_vma=False,
    )
```

```python
import functools

import jax
import jax.numpy as jnp
from jax import lax
from jax.experimental import pallas as pl
from jax.experimental.pallas import tpu as pltpu
from jax.sharding import PartitionSpec as P

MESH = pl.DeviceIdType.MESH
NT = (((1,), (1,)), ((), ()))
TN = (((0,), (0,)), ((), ()))


def factors(branch, side_row, gate_count):
    cuts = branch.shape[0]
    across = lax.broadcasted_iota(jnp.int32, (cuts, cuts), 0)
    down = lax.broadcasted_iota(jnp.int32, (cuts, cuts), 1)
    side = jnp.sum(jnp.where(across == down, side_row, 0.0), axis=1, keepdims=True)
    place = lax.broadcasted_iota(jnp.int32, (cuts, gate_count), 0)
    code = lax.broadcasted_iota(jnp.int32, (cuts, gate_count), 1)
    bits = (jnp.right_shift(code, place) & 1).astype(jnp.float32)

    def dot(columns, table):
        return lax.dot_general(
            columns.astype(jnp.bfloat16), table.astype(jnp.bfloat16), TN,
            preferred_element_type=jnp.float32,
        )

    made = []
    for projector in (side, 1.0 - side):
        chosen = branch * projector
        misses = dot(chosen, 1.0 - bits) + dot(projector - chosen, bits)
        parity = dot(branch - chosen, bits).astype(jnp.int32) & 1
        sign = (1 - 2 * parity).astype(jnp.float32)
        made.append(jnp.where(misses == 0.0, sign, 0.0))
    return made


def one_hot(which, path_map):
    return jnp.where(which == path_map, 1.0, 0.0).T.astype(jnp.bfloat16)


def picked_rows(hot, prefix):
    gate_count = prefix.shape[-1]
    rows = prefix.astype(jnp.float32).reshape(-1, gate_count).astype(jnp.bfloat16)
    return jnp.dot(hot, rows, preferred_element_type=jnp.float32)


def kernel(
    sizes,
    left_prefix, right_prefix, left_layer, right_layer, left_map, right_map, branch_bits, cut_side,
    left_out, right_out,
    left_rows, right_rows, left_proj, right_factor, right_proj, left_w, right_w,
    left_st, right_st, stage, hot_l, hot_r,
    own_sem, pre_send, pre_recv,
    pz_send, pz_recv, ps_send, ps_recv,
    st_send, st_recv, ss_send, ss_recv,
    l_send, l_recv, l_sib_send, l_sib_recv, o_send, o_recv, lo_sem, ro_sem,
):
    n_half, n_path, n_tile = sizes
    x, z, c = lax.axis_index("half"), lax.axis_index("path"), lax.axis_index("tile")
    sib = 1 - c
    n_lr = n_half * n_tile
    mine = x * n_tile + c

    barrier = pltpu.get_barrier_semaphore()

    def chips(do):
        for dz in range(n_path - 1, -1, -1):
            for dx in range(n_half):
                if dz or dx:
                    do(lax.rem(x + dx, n_half), lax.rem(z + dz, n_path))

    chips(lambda tx, tz: pl.semaphore_signal(
        barrier, inc=1, device_id={"half": tx, "path": tz}, device_id_type=MESH
    ))
    pl.semaphore_signal(barrier, inc=1, device_id={"tile": sib}, device_id_type=MESH)

    block_l, gate = left_layer.shape
    block_r = right_layer.shape[0]
    part_r = block_r // n_tile
    chunk_l = max(16, block_l // 4)
    count_l = block_l // chunk_l

    own = [
        pltpu.make_async_copy(left_prefix, left_rows.at[z], own_sem.at[0]),
        pltpu.make_async_copy(right_prefix, right_rows.at[z, c, x], own_sem.at[1]),
        pltpu.make_async_copy(
            left_layer, left_w.at[pl.ds(pl.multiple_of(mine * block_l, block_l), block_l)], own_sem.at[2]
        ),
        pltpu.make_async_copy(right_layer, right_w, own_sem.at[3]),
    ]
    for copy in own:
        copy.start()

    pl.semaphore_wait(barrier, n_path * n_half)

    def remote(src, dst, send, recv, device):
        return pltpu.make_async_remote_copy(
            src_ref=src, dst_ref=dst, send_sem=send, recv_sem=recv, device_id=device, device_id_type=MESH
        )

    def prefix_out(tx, tz):
        return remote(
            right_prefix, right_rows.at[z, c, x], pz_send.at[tz * n_half + tx],
            pz_recv.at[z * n_half + x], {"half": tx, "path": tz},
        )

    def prefix_in(fx, fz):
        held = right_rows.at[fz, c, fx]
        return remote(
            held, held, pz_send.at[fz * n_half + fx], pz_recv.at[fz * n_half + fx],
            {"half": fx, "path": fz},
        )

    chips(lambda tx, tz: prefix_out(tx, tz).start())
    prefix_copies = [
        remote(
            left_prefix, left_rows.at[z], pre_send.at[k - 1], pre_recv.at[k - 1],
            {"path": lax.rem(z + k, n_path)},
        )
        for k in range(1, n_path)
    ]
    for copy in prefix_copies:
        copy.start()

    def rows_l(block, core, i):
        return pl.ds(
            pl.multiple_of((block * n_tile + core) * block_l + i * chunk_l, chunk_l), chunk_l
        )

    def left_flush(block, core, i):
        span = rows_l(block, core, i)
        at = (block * n_tile + core) * count_l + i
        return pltpu.make_async_copy(left_st.at[span], left_out.at[span], lo_sem.at[at])

    def part(block, core):
        return pl.ds(pl.multiple_of(block * block_r + core * part_r, part_r), part_r)

    def right_flush(block, core):
        span = part(block, core)
        return pltpu.make_async_copy(
            right_st.at[span], right_out.at[span], ro_sem.at[block * n_tile + core]
        )

    class Line:
        def __init__(self, axis, pos, n, rows, buf, first, proj, count, sems):
            self.axis, self.pos, self.n, self.rows, self.buf = axis, pos, n, rows, buf
            self.first, self.proj, self.count = first, proj, count
            self.send, self.recv, self.sib_send, self.sib_recv = sems
            self.slots = (n - 1) * count

        def block(self, way, d):
            return self.pos - d if way == 0 else self.pos + d

        def has(self, way, d):
            return (self.pos >= d) if way == 0 else (self.pos + d < self.n)

        def sends(self, way, d):
            onward = (self.pos + 1 < self.n) if way == 0 else (self.pos >= 1)
            return jnp.logical_and(self.has(way, d), onward)

        def onward(self, way, d, i, own=False):
            span = self.rows(self.block(way, d), c, i)
            src = self.first(i) if own else self.buf.at[span]
            at = d * self.count + i
            return remote(
                src, self.buf.at[span], self.send.at[way, at], self.recv.at[way, at],
                {self.axis: self.pos + (1 if way == 0 else -1)},
            )

        def arrived(self, way, d, i):
            span = self.rows(self.block(way, d), c, i)
            at = (d - 1) * self.count + i
            return remote(
                self.buf.at[span], self.buf.at[span], self.send.at[way, at], self.recv.at[way, at],
                {self.axis: self.pos + (1 if way == 0 else -1)},
            )

        def share(self, way, d, i, core):
            span = self.rows(self.block(way, d), core, i)
            at = (d - 1) * self.count + i
            return remote(
                self.buf.at[span], self.buf.at[span],
                self.sib_send.at[way, at], self.sib_recv.at[way, at], {"tile": sib},
            )

        def start_own(self, i):
            for way in (0, 1):
                @pl.when(self.sends(way, 0))
                def _():
                    self.onward(way, 0, i, own=True).start()

        def relay(self, s):
            d, i = s // self.count + 1, lax.rem(s, self.count)
            for way in (0, 1):
                @pl.when(jnp.logical_and(s < self.slots, self.has(way, d)))
                def _():
                    self.arrived(way, d, i).wait_recv()
                    @pl.when(jnp.logical_and(self.sends(way, d), d < self.n - 1))
                    def _():
                        self.onward(way, d, i).start()
                    self.share(way, d, i, c).start()

        def multiply(self, block, core, i):
            span = self.rows(block, core, i)
            left_st[span, :] = lax.dot_general(
                self.buf[span, :], self.proj[...], NT, preferred_element_type=jnp.float32
            ).astype(jnp.bfloat16)
            left_flush(block, core, i).start()

        def compute(self, s):
            d, i = s // self.count + 1, lax.rem(s, self.count)
            for way in (0, 1):
                @pl.when(jnp.logical_and(s < self.slots, self.has(way, d)))
                def _():
                    self.multiply(self.block(way, d), c, i)

        def compute_shared(self, s):
            d, i = s // self.count + 1, lax.rem(s, self.count)
            for way in (0, 1):
                @pl.when(jnp.logical_and(jnp.logical_and(s >= 0, s < self.slots), self.has(way, d)))
                def _():
                    self.share(way, d, i, sib).wait_recv()
                    self.multiply(self.block(way, d), sib, i)

        def finish(self, s):
            d, i = s // self.count, lax.rem(s, self.count)
            for way in (0, 1):
                @pl.when(self.sends(way, d))
                def _():
                    self.onward(way, d, i).wait_send()
                @pl.when(self.has(way, d + 1))
                def _():
                    self.share(way, d + 1, i, c).wait_send()

    left = Line(
        "half", x, n_half, rows_l, left_w,
        lambda i: left_layer.at[pl.ds(i * chunk_l, chunk_l)],
        left_proj, count_l, (l_send, l_recv, l_sib_send, l_sib_recv),
    )

    def own_share(i, core):
        span = rows_l(x, core, i)
        return remote(
            left.first(i), left_w.at[span], o_send.at[i], o_recv.at[i], {"tile": sib}
        )

    for i in range(count_l):
        left.start_own(i)
    for i in range(count_l):
        own_share(i, c).start()

    side = cut_side[...].astype(jnp.float32)
    branch = branch_bits[...].astype(jnp.float32)
    for ref, factor in zip((left_proj, right_factor), factors(branch, side, gate)):
        ref[...] = factor.astype(jnp.bfloat16)

    shard = left_prefix.shape[0]
    paths = left_map.shape[1]
    hot_l[...] = one_hot(
        lax.broadcasted_iota(jnp.int32, (n_path * shard, paths), 0), left_map[...]
    )
    shard = right_prefix.shape[0]
    dims = (n_tile, n_half, shard, paths)
    core_at, half_at, row_at = (lax.broadcasted_iota(jnp.int32, dims, k) for k in range(3))
    which = (half_at * n_tile + core_at) * shard + row_at
    hot_r[...] = one_hot(which.reshape(n_lr * shard, paths), right_map[...])

    def prefix_share(block, core):
        held = right_rows.at[block, core]
        return remote(held, held, ps_send.at[block], ps_recv.at[block], {"tile": sib})

    def state_out(to):
        return remote(
            stage.at[to], right_st.at[part(z, c)], st_send.at[to], st_recv.at[z], {"path": to}
        )

    def state_in(block):
        return remote(
            stage.at[block], right_st.at[part(block, c)], st_send.at[block], st_recv.at[block],
            {"path": block},
        )

    def state_share(block, core):
        held = right_st.at[part(block, core)]
        return remote(held, held, ss_send.at[block], ss_recv.at[block], {"tile": sib})

    def each(d, do):
        @pl.when(z >= d)
        def _():
            do(z - d)
        @pl.when(z + d < n_path)
        def _():
            do(z + d)

    own[1].wait()
    for dx in range(1, n_half):
        prefix_in(lax.rem(x + dx, n_half), z).wait_recv()
    prefix_share(z, c).start()

    def project_right(block):
        chosen = picked_rows(hot_r[...], right_rows[block])
        right_proj[...] = (chosen * right_factor[...].astype(jnp.float32)).astype(jnp.bfloat16)

    def right_times(rows):
        return lax.dot_general(
            rows, right_proj[...], NT, preferred_element_type=jnp.float32
        ).astype(jnp.bfloat16)

    own[0].wait()
    for copy in prefix_copies:
        copy.wait_recv()
    chosen = picked_rows(hot_l[...], left_rows[...])
    left_proj[...] = (chosen * left_proj[...].astype(jnp.float32)).astype(jnp.bfloat16)
    own[2].wait()
    own[3].wait()

    def right_step(d):
        def pass_on(block):
            for fx in range(n_half):
                prefix_in(fx, block).wait_recv()
            prefix_share(block, c).start()
        each(d, pass_on)

        def form(block):
            prefix_share(block, sib).wait_recv()
            project_right(block)
            stage[block] = right_times(right_w[pl.ds(pl.multiple_of(c * part_r, part_r), part_r), :])
            state_out(block).start()
        each(d, form)

    def left_step(s):
        left.relay(s)
        left.compute_shared(s - 1)
        left.compute(s)

    prefix_share(z, sib).wait_recv()
    project_right(z)
    for core in range(n_tile):
        right_st[part(z, core), :] = right_times(right_w[core * part_r:(core + 1) * part_r, :])
        right_flush(z, core).start()
    for i in range(count_l):
        left.multiply(x, c, i)

    steps = max(n_path - 1, left.slots)

    def step(t, _):
        @pl.when(t < n_path - 1)
        def _():
            right_step(t + 1)
        left_step(t)
        return 0

    def shared_block():
        for i in range(count_l):
            own_share(i, sib).wait_recv()
            left.multiply(x, sib, i)

    shared_block()
    both = min(n_path - 1, left.slots)
    if both > 0:
        lax.fori_loop(0, both, step, 0)
    if n_path - 1 > both:
        lax.fori_loop(both, n_path - 1, lambda t, _: (right_step(t + 1), 0)[1], 0)

    def take(k, _):
        def landed(block):
            state_in(block).wait_recv()
            state_share(block, c).start()
            right_flush(block, c).start()
        each(k + 1, landed)
        return 0

    if n_path > 1:
        lax.fori_loop(0, n_path - 1, take, 0)
    if left.slots > both:
        lax.fori_loop(both, left.slots, lambda t, _: (left_step(t), 0)[1], 0)

    def take_shared(k, _):
        def landed(block):
            state_share(block, sib).wait_recv()
            right_flush(block, sib).start()
        each(k + 1, landed)
        return 0

    if n_path > 1:
        lax.fori_loop(0, n_path - 1, take_shared, 0)
    left.compute_shared(jnp.int32(left.slots - 1))

    def close(k, _):
        def ended(block):
            prefix_share(block, c).wait_send()
            state_out(block).wait_send()
            state_share(block, c).wait_send()
        each(k + 1, ended)
        return 0

    if n_path > 1:
        lax.fori_loop(0, n_path - 1, close, 0)
    if left.slots > 0:
        lax.fori_loop(0, left.slots, lambda s, _: (left.finish(s), 0)[1], 0)
    for i in range(count_l):
        own_share(i, c).wait_send()
    chips(lambda tx, tz: prefix_out(tx, tz).wait_send())
    prefix_share(z, c).wait_send()
    for copy in prefix_copies:
        copy.wait_send()

    def flushed_left(k, _):
        for core in range(n_tile):
            for i in range(count_l):
                left_flush(k, core, i).wait()
        return 0

    def flushed_right(k, _):
        for core in range(n_tile):
            right_flush(k, core).wait()
        return 0

    lax.fori_loop(0, n_half, flushed_left, 0)
    lax.fori_loop(0, n_path, flushed_right, 0)


def on_device(
    sizes,
    left_prefix, right_prefix, left_layer, right_layer, left_map, right_map, branch_bits, cut_side,
):
    n_half, n_path, n_tile = sizes
    n_lr = n_half * n_tile
    paths = left_map.shape[0]
    gate = left_layer.shape[1]
    hi_l, hi_r = left_layer.shape[0] * n_lr, right_layer.shape[0] * n_path
    part_r = right_layer.shape[0] // n_tile
    count_l = left_layer.shape[0] // max(16, left_layer.shape[0] // 4)
    slots_l = max(1, (n_half - 1) * count_l)
    pre = max(1, n_path - 1)
    chips = n_path * n_half
    dma = pltpu.SemaphoreType.DMA
    vmem = pl.BlockSpec(memory_space=pltpu.VMEM)
    anywhere = pl.BlockSpec(memory_space=pl.ANY)
    left_states, right_states = pl.pallas_call(
        functools.partial(kernel, sizes),
        out_shape=(
            jax.ShapeDtypeStruct((hi_l, paths), jnp.bfloat16),
            jax.ShapeDtypeStruct((hi_r, paths), jnp.bfloat16),
        ),
        in_specs=[anywhere] * 4 + [vmem] * 4,
        out_specs=(anywhere, anywhere),
        scratch_shapes=[
            pltpu.VMEM((n_path,) + left_prefix.shape, jnp.bfloat16),
            pltpu.VMEM((n_path, n_tile, n_half) + right_prefix.shape, jnp.bfloat16),
            pltpu.VMEM((paths, gate), jnp.bfloat16),
            pltpu.VMEM((paths, gate), jnp.bfloat16),
            pltpu.VMEM((paths, gate), jnp.bfloat16),
            pltpu.VMEM((hi_l, gate), jnp.bfloat16),
            pltpu.VMEM(right_layer.shape, jnp.bfloat16),
            pltpu.VMEM((hi_l, paths), jnp.bfloat16),
            pltpu.VMEM((hi_r, paths), jnp.bfloat16),
            pltpu.VMEM((n_path, part_r, paths), jnp.bfloat16),
            pltpu.VMEM((paths, left_prefix.shape[0] * n_path), jnp.bfloat16),
            pltpu.VMEM((paths, right_prefix.shape[0] * n_lr), jnp.bfloat16),
            dma((4,)), dma((pre,)), dma((pre,)),
            dma((chips,)), dma((chips,)),
        ] + [dma((n_path,))] * 6 + [
            dma((2, slots_l)), dma((2, slots_l)), dma((2, slots_l)), dma((2, slots_l)),
            dma((count_l,)), dma((count_l,)),
            dma((n_lr * count_l,)), dma((n_path * n_tile,)),
        ],
        compiler_params=pltpu.CompilerParams(collective_id=0, has_side_effects=True),
    )(
        left_prefix, right_prefix, left_layer, right_layer,
        left_map[None, :], right_map[None, :], branch_bits.T, cut_side[None, :],
    )
    amplitude = lax.dot_general(
        left_states, right_states, NT, preferred_element_type=jnp.float32
    )
    return amplitude.astype(jnp.bfloat16)


def solution(mesh):
    in_specs = (
        P(("groups", "path"), ("half", "tile")),
        P(("groups", "half", "tile"), "path"),
        P(("groups", "half", "tile"), None),
        P(("groups", "path"), None),
        P("groups"),
        P("groups"),
        P("groups", None),
        P("groups"),
    )
    out_specs = P(("groups", "half", "tile"), "path")
    sizes = tuple(mesh.shape[axis] for axis in ("half", "path", "tile"))
    return jax.shard_map(
        functools.partial(on_device, sizes),
        mesh=mesh, in_specs=in_specs, out_specs=out_specs, check_vma=False,
    )
```

```python
import functools

import jax
import jax.numpy as jnp
from jax import lax
from jax.experimental import pallas as pl
from jax.experimental.pallas import tpu as pltpu
from jax.sharding import PartitionSpec as P

MESH = pl.DeviceIdType.MESH
NT = (((1,), (1,)), ((), ()))
TN = (((0,), (0,)), ((), ()))


def factors(branch, side_row, gate_count):
    cuts = branch.shape[0]
    across = lax.broadcasted_iota(jnp.int32, (cuts, cuts), 0)
    down = lax.broadcasted_iota(jnp.int32, (cuts, cuts), 1)
    side = jnp.sum(jnp.where(across == down, side_row, 0.0), axis=1, keepdims=True)
    place = lax.broadcasted_iota(jnp.int32, (cuts, gate_count), 0)
    code = lax.broadcasted_iota(jnp.int32, (cuts, gate_count), 1)
    bits = (jnp.right_shift(code, place) & 1).astype(jnp.float32)

    def dot(columns, table):
        return lax.dot_general(
            columns.astype(jnp.bfloat16), table.astype(jnp.bfloat16), TN,
            preferred_element_type=jnp.float32,
        )

    made = []
    for projector in (side, 1.0 - side):
        chosen = branch * projector
        misses = dot(chosen, 1.0 - bits) + dot(projector - chosen, bits)
        parity = dot(branch - chosen, bits).astype(jnp.int32) & 1
        sign = (1 - 2 * parity).astype(jnp.float32)
        made.append(jnp.where(misses == 0.0, sign, 0.0))
    return made


def one_hot(rows, path_map):
    which = lax.broadcasted_iota(jnp.int32, (rows, path_map.shape[1]), 0)
    return jnp.where(which == path_map, 1.0, 0.0).T.astype(jnp.bfloat16)


def picked_rows(hot, prefix):
    gate_count = prefix.shape[-1]
    rows = prefix.astype(jnp.float32).reshape(-1, gate_count).astype(jnp.bfloat16)
    return jnp.dot(hot, rows, preferred_element_type=jnp.float32)


def kernel(
    sizes,
    left_prefix, right_prefix, left_layer, right_layer, left_map, right_map, branch_bits, cut_side,
    left_out, right_out,
    left_rows, right_rows, left_proj, right_factor, right_proj, left_w, right_w,
    left_st, right_st, stage, hot_l, hot_r, told,
    own_sem, pre_send, pre_recv,
    pz_send, pz_recv, ps_send, ps_recv,
    st_send, st_recv, ss_send, ss_recv,
    l_send, l_recv, l_sib_send, l_sib_recv, o_send, o_recv, lo_sem, ro_sem,
):
    n_half, n_path, n_tile = sizes
    x, z, c = lax.axis_index("half"), lax.axis_index("path"), lax.axis_index("tile")
    sib = 1 - c
    n_lr = n_half * n_tile
    mine = x * n_tile + c

    barrier = pltpu.get_barrier_semaphore()
    def neighbours(do):
        @pl.when(z >= 1)
        def _():
            do(z - 1, 1)
        @pl.when(z + 1 < n_path)
        def _():
            do(z + 1, 0)

    neighbours(lambda there, _: pl.semaphore_signal(
        barrier, inc=1, device_id={"path": there}, device_id_type=MESH
    ))
    for k in range(1, n_lr):
        there = lax.rem(mine + k, n_lr)
        pl.semaphore_signal(
            barrier,
            inc=1,
            device_id={"half": there // n_tile, "tile": lax.rem(there, n_tile)},
            device_id_type=MESH,
        )

    block_l, gate = left_layer.shape
    block_r = right_layer.shape[0]
    part_r = block_r // n_tile
    chunk_l = max(16, block_l // 4)
    count_l = block_l // chunk_l
    half_lr = n_lr // n_tile

    own = [
        pltpu.make_async_copy(left_prefix, left_rows.at[z], own_sem.at[0]),
        pltpu.make_async_copy(right_prefix, right_rows.at[z, mine], own_sem.at[1]),
        pltpu.make_async_copy(
            left_layer, left_w.at[pl.ds(pl.multiple_of(mine * block_l, block_l), block_l)], own_sem.at[2]
        ),
        pltpu.make_async_copy(right_layer, right_w, own_sem.at[3]),
    ]
    for copy in own:
        copy.start()

    side = cut_side[...].astype(jnp.float32)
    branch = branch_bits[...].astype(jnp.float32)
    for ref, factor in zip((left_proj, right_factor), factors(branch, side, gate)):
        ref[...] = factor.astype(jnp.bfloat16)

    beside = (z >= 1).astype(jnp.int32) + (z + 1 < n_path).astype(jnp.int32)
    pl.semaphore_wait(barrier, beside + n_lr - 1)

    def tell():
        neighbours(lambda there, way: pl.semaphore_signal(
            told.at[way], inc=1, device_id={"path": there}, device_id_type=MESH
        ))

    def hear():
        @pl.when(z >= 1)
        def _():
            pl.semaphore_wait(told.at[0], 1)
        @pl.when(z + 1 < n_path)
        def _():
            pl.semaphore_wait(told.at[1], 1)

    if n_path > 2:
        tell()

    def remote(src, dst, send, recv, device):
        return pltpu.make_async_remote_copy(
            src_ref=src, dst_ref=dst, send_sem=send, recv_sem=recv, device_id=device, device_id_type=MESH
        )

    prefix_copies = []
    for k in range(1, n_path):
        prefix_copies.append(remote(
            left_prefix, left_rows.at[z], pre_send.at[k - 1], pre_recv.at[k - 1],
            {"path": lax.rem(z + k, n_path)},
        ))
    for k in range(1, n_lr):
        there = lax.rem(mine + k, n_lr)
        slot = n_path - 1 + k - 1
        prefix_copies.append(remote(
            right_prefix, right_rows.at[z, mine], pre_send.at[slot], pre_recv.at[slot],
            {"half": there // n_tile, "tile": lax.rem(there, n_tile)},
        ))
    for copy in prefix_copies[n_path - 1:]:
        copy.start()

    def rows_l(block, core, i):
        return pl.ds(
            pl.multiple_of((block * n_tile + core) * block_l + i * chunk_l, chunk_l), chunk_l
        )

    def left_flush(block, core, i):
        span = rows_l(block, core, i)
        at = (block * n_tile + core) * count_l + i
        return pltpu.make_async_copy(left_st.at[span], left_out.at[span], lo_sem.at[at])

    def part(block, core):
        return pl.ds(pl.multiple_of(block * block_r + core * part_r, part_r), part_r)

    def right_flush(block, core):
        span = part(block, core)
        return pltpu.make_async_copy(
            right_st.at[span], right_out.at[span], ro_sem.at[block * n_tile + core]
        )

    class Line:
        def __init__(self, axis, pos, n, rows, buf, first, proj, count, sems):
            self.axis, self.pos, self.n, self.rows, self.buf = axis, pos, n, rows, buf
            self.first, self.proj, self.count = first, proj, count
            self.send, self.recv, self.sib_send, self.sib_recv = sems
            self.slots = (n - 1) * count

        def block(self, way, d):
            return self.pos - d if way == 0 else self.pos + d

        def has(self, way, d):
            return (self.pos >= d) if way == 0 else (self.pos + d < self.n)

        def sends(self, way, d):
            onward = (self.pos + 1 < self.n) if way == 0 else (self.pos >= 1)
            return jnp.logical_and(self.has(way, d), onward)

        def onward(self, way, d, i, own=False):
            span = self.rows(self.block(way, d), c, i)
            src = self.first(i) if own else self.buf.at[span]
            at = d * self.count + i
            return remote(
                src, self.buf.at[span], self.send.at[way, at], self.recv.at[way, at],
                {self.axis: self.pos + (1 if way == 0 else -1)},
            )

        def arrived(self, way, d, i):
            span = self.rows(self.block(way, d), c, i)
            at = (d - 1) * self.count + i
            return remote(
                self.buf.at[span], self.buf.at[span], self.send.at[way, at], self.recv.at[way, at],
                {self.axis: self.pos + (1 if way == 0 else -1)},
            )

        def share(self, way, d, i, core):
            span = self.rows(self.block(way, d), core, i)
            at = (d - 1) * self.count + i
            return remote(
                self.buf.at[span], self.buf.at[span],
                self.sib_send.at[way, at], self.sib_recv.at[way, at], {"tile": sib},
            )

        def start_own(self, i):
            for way in (0, 1):
                @pl.when(self.sends(way, 0))
                def _():
                    self.onward(way, 0, i, own=True).start()

        def relay(self, s):
            d, i = s // self.count + 1, lax.rem(s, self.count)
            for way in (0, 1):
                @pl.when(jnp.logical_and(s < self.slots, self.has(way, d)))
                def _():
                    self.arrived(way, d, i).wait_recv()
                    @pl.when(jnp.logical_and(self.sends(way, d), d < self.n - 1))
                    def _():
                        self.onward(way, d, i).start()
                    self.share(way, d, i, c).start()

        def multiply(self, block, core, i):
            span = self.rows(block, core, i)
            left_st[span, :] = lax.dot_general(
                self.buf[span, :], self.proj[...], NT, preferred_element_type=jnp.float32
            ).astype(jnp.bfloat16)
            left_flush(block, core, i).start()

        def compute(self, s):
            d, i = s // self.count + 1, lax.rem(s, self.count)
            for way in (0, 1):
                @pl.when(jnp.logical_and(s < self.slots, self.has(way, d)))
                def _():
                    self.multiply(self.block(way, d), c, i)

        def compute_shared(self, s):
            d, i = s // self.count + 1, lax.rem(s, self.count)
            for way in (0, 1):
                @pl.when(jnp.logical_and(jnp.logical_and(s >= 0, s < self.slots), self.has(way, d)))
                def _():
                    self.share(way, d, i, sib).wait_recv()
                    self.multiply(self.block(way, d), sib, i)

        def finish(self, s):
            d, i = s // self.count, lax.rem(s, self.count)
            for way in (0, 1):
                @pl.when(self.sends(way, d))
                def _():
                    self.onward(way, d, i).wait_send()
                @pl.when(self.has(way, d + 1))
                def _():
                    self.share(way, d + 1, i, c).wait_send()

    left = Line(
        "half", x, n_half, rows_l, left_w,
        lambda i: left_layer.at[pl.ds(i * chunk_l, chunk_l)],
        left_proj, count_l, (l_send, l_recv, l_sib_send, l_sib_recv),
    )

    def own_share(i, core):
        span = rows_l(x, core, i)
        return remote(
            left.first(i), left_w.at[span], o_send.at[i], o_recv.at[i], {"tile": sib}
        )

    for i in range(count_l):
        left.start_own(i)
    for i in range(count_l):
        own_share(i, c).start()

    hot_l[...] = one_hot(hot_l.shape[1], left_map[...])
    hot_r[...] = one_hot(hot_r.shape[1], right_map[...])
    if n_path > 2:
        hear()
        for _ in range(n_path - 3):
            tell()
            hear()
    for copy in prefix_copies[:n_path - 1]:
        copy.start()

    def prefix_half(block, core):
        return right_rows.at[block, pl.ds(core * half_lr, half_lr)]

    def prefix_out(to):
        held = prefix_half(z, c)
        return remote(held, held, pz_send.at[to], pz_recv.at[z], {"path": to})

    def prefix_in(block):
        held = prefix_half(block, c)
        return remote(held, held, pz_send.at[block], pz_recv.at[block], {"path": block})

    def prefix_share(block, core):
        held = prefix_half(block, core)
        return remote(held, held, ps_send.at[block], ps_recv.at[block], {"tile": sib})

    def state_out(to):
        return remote(
            stage.at[to], right_st.at[part(z, c)], st_send.at[to], st_recv.at[z], {"path": to}
        )

    def state_in(block):
        return remote(
            stage.at[block], right_st.at[part(block, c)], st_send.at[block], st_recv.at[block],
            {"path": block},
        )

    def state_share(block, core):
        held = right_st.at[part(block, core)]
        return remote(held, held, ss_send.at[block], ss_recv.at[block], {"tile": sib})

    def each(d, do):
        @pl.when(z >= d)
        def _():
            do(z - d)
        @pl.when(z + d < n_path)
        def _():
            do(z + d)

    own[1].wait()
    for copy in prefix_copies[n_path - 1:]:
        copy.wait_recv()
    def far_first(k, _):
        each(n_path - 1 - k, lambda to: prefix_out(to).start())
        return 0
    if n_path > 1:
        lax.fori_loop(0, n_path - 1, far_first, 0)

    def project_right(block):
        chosen = picked_rows(hot_r[...], right_rows[block])
        right_proj[...] = (chosen * right_factor[...].astype(jnp.float32)).astype(jnp.bfloat16)

    def right_times(rows):
        return lax.dot_general(
            rows, right_proj[...], NT, preferred_element_type=jnp.float32
        ).astype(jnp.bfloat16)

    own[0].wait()
    for copy in prefix_copies[:n_path - 1]:
        copy.wait_recv()
    chosen = picked_rows(hot_l[...], left_rows[...])
    left_proj[...] = (chosen * left_proj[...].astype(jnp.float32)).astype(jnp.bfloat16)
    own[2].wait()
    own[3].wait()

    def right_step(d):
        def pass_on(block):
            prefix_in(block).wait_recv()
            prefix_share(block, c).start()
        each(d, pass_on)

        def form(block):
            prefix_share(block, sib).wait_recv()
            project_right(block)
            stage[block] = right_times(right_w[pl.ds(pl.multiple_of(c * part_r, part_r), part_r), :])
            state_out(block).start()
        each(d, form)

    def left_step(s):
        left.relay(s)
        left.compute_shared(s - 1)
        left.compute(s)

    project_right(z)
    for core in range(n_tile):
        right_st[part(z, core), :] = right_times(right_w[core * part_r:(core + 1) * part_r, :])
        right_flush(z, core).start()
    for i in range(count_l):
        left.multiply(x, c, i)

    steps = max(n_path - 1, left.slots)

    def step(t, _):
        @pl.when(t < n_path - 1)
        def _():
            right_step(t + 1)
        left_step(t)
        return 0

    def shared_block():
        for i in range(count_l):
            own_share(i, sib).wait_recv()
            left.multiply(x, sib, i)

    shared_block()
    both = min(n_path - 1, left.slots)
    if both > 0:
        lax.fori_loop(0, both, step, 0)
    if n_path - 1 > both:
        lax.fori_loop(both, n_path - 1, lambda t, _: (right_step(t + 1), 0)[1], 0)

    def take(k, _):
        def landed(block):
            state_in(block).wait_recv()
            state_share(block, c).start()
            right_flush(block, c).start()
        each(k + 1, landed)
        return 0

    if n_path > 1:
        lax.fori_loop(0, n_path - 1, take, 0)
    if left.slots > both:
        lax.fori_loop(both, left.slots, lambda t, _: (left_step(t), 0)[1], 0)

    def take_shared(k, _):
        def landed(block):
            state_share(block, sib).wait_recv()
            right_flush(block, sib).start()
        each(k + 1, landed)
        return 0

    if n_path > 1:
        lax.fori_loop(0, n_path - 1, take_shared, 0)
    left.compute_shared(jnp.int32(left.slots - 1))

    def close(k, _):
        def ended(block):
            prefix_out(block).wait_send()
            prefix_share(block, c).wait_send()
            state_out(block).wait_send()
            state_share(block, c).wait_send()
        each(k + 1, ended)
        return 0

    if n_path > 1:
        lax.fori_loop(0, n_path - 1, close, 0)
    if left.slots > 0:
        lax.fori_loop(0, left.slots, lambda s, _: (left.finish(s), 0)[1], 0)
    for i in range(count_l):
        own_share(i, c).wait_send()
    for copy in prefix_copies:
        copy.wait_send()

    def flushed_left(k, _):
        for core in range(n_tile):
            for i in range(count_l):
                left_flush(k, core, i).wait()
        return 0

    def flushed_right(k, _):
        for core in range(n_tile):
            right_flush(k, core).wait()
        return 0

    lax.fori_loop(0, n_half, flushed_left, 0)
    lax.fori_loop(0, n_path, flushed_right, 0)


def on_device(
    sizes,
    left_prefix, right_prefix, left_layer, right_layer, left_map, right_map, branch_bits, cut_side,
):
    n_half, n_path, n_tile = sizes
    n_lr = n_half * n_tile
    paths = left_map.shape[0]
    gate = left_layer.shape[1]
    hi_l, hi_r = left_layer.shape[0] * n_lr, right_layer.shape[0] * n_path
    part_r = right_layer.shape[0] // n_tile
    count_l = left_layer.shape[0] // max(16, left_layer.shape[0] // 4)
    slots_l = max(1, (n_half - 1) * count_l)
    pre = n_path + n_lr - 2
    dma = pltpu.SemaphoreType.DMA
    vmem = pl.BlockSpec(memory_space=pltpu.VMEM)
    anywhere = pl.BlockSpec(memory_space=pl.ANY)
    left_states, right_states = pl.pallas_call(
        functools.partial(kernel, sizes),
        out_shape=(
            jax.ShapeDtypeStruct((hi_l, paths), jnp.bfloat16),
            jax.ShapeDtypeStruct((hi_r, paths), jnp.bfloat16),
        ),
        in_specs=[anywhere] * 4 + [vmem] * 4,
        out_specs=(anywhere, anywhere),
        scratch_shapes=[
            pltpu.VMEM((n_path,) + left_prefix.shape, jnp.bfloat16),
            pltpu.VMEM((n_path, n_lr) + right_prefix.shape, jnp.bfloat16),
            pltpu.VMEM((paths, gate), jnp.bfloat16),
            pltpu.VMEM((paths, gate), jnp.bfloat16),
            pltpu.VMEM((paths, gate), jnp.bfloat16),
            pltpu.VMEM((hi_l, gate), jnp.bfloat16),
            pltpu.VMEM(right_layer.shape, jnp.bfloat16),
            pltpu.VMEM((hi_l, paths), jnp.bfloat16),
            pltpu.VMEM((hi_r, paths), jnp.bfloat16),
            pltpu.VMEM((n_path, part_r, paths), jnp.bfloat16),
            pltpu.VMEM((paths, left_prefix.shape[0] * n_path), jnp.bfloat16),
            pltpu.VMEM((paths, right_prefix.shape[0] * n_lr), jnp.bfloat16),
            pltpu.SemaphoreType.REGULAR((2,)),
            dma((4,)), dma((pre,)), dma((pre,)),
        ] + [dma((n_path,))] * 8 + [
            dma((2, slots_l)), dma((2, slots_l)), dma((2, slots_l)), dma((2, slots_l)),
            dma((count_l,)), dma((count_l,)),
            dma((n_lr * count_l,)), dma((n_path * n_tile,)),
        ],
        compiler_params=pltpu.CompilerParams(collective_id=0, has_side_effects=True),
    )(
        left_prefix, right_prefix, left_layer, right_layer,
        left_map[None, :], right_map[None, :], branch_bits.T, cut_side[None, :],
    )
    amplitude = lax.dot_general(
        left_states, right_states, NT, preferred_element_type=jnp.float32
    )
    return amplitude.astype(jnp.bfloat16)


def solution(mesh):
    in_specs = (
        P(("groups", "path"), ("half", "tile")),
        P(("groups", "half", "tile"), "path"),
        P(("groups", "half", "tile"), None),
        P(("groups", "path"), None),
        P("groups"),
        P("groups"),
        P("groups", None),
        P("groups"),
    )
    out_specs = P(("groups", "half", "tile"), "path")
    sizes = tuple(mesh.shape[axis] for axis in ("half", "path", "tile"))
    return jax.shard_map(
        functools.partial(on_device, sizes),
        mesh=mesh, in_specs=in_specs, out_specs=out_specs, check_vma=False,
    )
```

```python
import functools

import jax
import jax.numpy as jnp
from jax import lax
from jax.experimental import pallas as pl
from jax.experimental.pallas import tpu as pltpu
from jax.sharding import PartitionSpec as P

MESH = pl.DeviceIdType.MESH
NT = (((1,), (1,)), ((), ()))
TN = (((0,), (0,)), ((), ()))


def factors(branch, side_row, gate_count):
    cuts = branch.shape[0]
    across = lax.broadcasted_iota(jnp.int32, (cuts, cuts), 0)
    down = lax.broadcasted_iota(jnp.int32, (cuts, cuts), 1)
    side = jnp.sum(jnp.where(across == down, side_row, 0.0), axis=1, keepdims=True)
    place = lax.broadcasted_iota(jnp.int32, (cuts, gate_count), 0)
    code = lax.broadcasted_iota(jnp.int32, (cuts, gate_count), 1)
    bits = (jnp.right_shift(code, place) & 1).astype(jnp.float32)

    def dot(columns, table):
        return lax.dot_general(
            columns.astype(jnp.bfloat16), table.astype(jnp.bfloat16), TN,
            preferred_element_type=jnp.float32,
        )

    made = []
    for projector in (side, 1.0 - side):
        chosen = branch * projector
        misses = dot(chosen, 1.0 - bits) + dot(projector - chosen, bits)
        parity = dot(branch - chosen, bits).astype(jnp.int32) & 1
        sign = (1 - 2 * parity).astype(jnp.float32)
        made.append(jnp.where(misses == 0.0, sign, 0.0))
    return made


def one_hot(rows, path_map):
    which = lax.broadcasted_iota(jnp.int32, (rows, path_map.shape[1]), 0)
    return jnp.where(which == path_map, 1.0, 0.0).T.astype(jnp.bfloat16)


def picked_rows(hot, prefix):
    gate_count = prefix.shape[-1]
    rows = prefix.astype(jnp.float32).reshape(-1, gate_count).astype(jnp.bfloat16)
    return jnp.dot(hot, rows, preferred_element_type=jnp.float32)


def kernel(
    sizes,
    left_prefix, right_prefix, left_layer, right_layer, left_map, right_map, branch_bits, cut_side,
    left_out, right_out,
    left_rows, right_rows, left_proj, right_factor, right_proj, left_w, right_w,
    left_st, right_st, stage, hot_l, hot_r, told,
    own_sem, pre_send, pre_recv,
    pz_send, pz_recv, ps_send, ps_recv,
    st_send, st_recv, ss_send, ss_recv,
    l_send, l_recv, l_sib_send, l_sib_recv, o_send, o_recv, lo_sem, ro_sem,
):
    n_half, n_path, n_tile = sizes
    x, z, c = lax.axis_index("half"), lax.axis_index("path"), lax.axis_index("tile")
    sib = 1 - c
    n_lr = n_half * n_tile
    mine = x * n_tile + c

    barrier = pltpu.get_barrier_semaphore()
    def neighbours(do):
        @pl.when(z >= 1)
        def _():
            do(z - 1, 1)
        @pl.when(z + 1 < n_path)
        def _():
            do(z + 1, 0)

    neighbours(lambda there, _: pl.semaphore_signal(
        barrier, inc=1, device_id={"path": there}, device_id_type=MESH
    ))
    for k in range(1, n_lr):
        there = lax.rem(mine + k, n_lr)
        pl.semaphore_signal(
            barrier,
            inc=1,
            device_id={"half": there // n_tile, "tile": lax.rem(there, n_tile)},
            device_id_type=MESH,
        )

    block_l, gate = left_layer.shape
    block_r = right_layer.shape[0]
    part_r = block_r // n_tile
    chunk_l = max(16, block_l // 4)
    count_l = block_l // chunk_l
    half_lr = n_lr // n_tile

    own = [
        pltpu.make_async_copy(left_prefix, left_rows.at[z], own_sem.at[0]),
        pltpu.make_async_copy(right_prefix, right_rows.at[z, mine], own_sem.at[1]),
        pltpu.make_async_copy(
            left_layer, left_w.at[pl.ds(pl.multiple_of(mine * block_l, block_l), block_l)], own_sem.at[2]
        ),
        pltpu.make_async_copy(right_layer, right_w, own_sem.at[3]),
    ]
    for copy in own:
        copy.start()

    side = cut_side[...].astype(jnp.float32)
    branch = branch_bits[...].astype(jnp.float32)
    for ref, factor in zip((left_proj, right_factor), factors(branch, side, gate)):
        ref[...] = factor.astype(jnp.bfloat16)

    beside = (z >= 1).astype(jnp.int32) + (z + 1 < n_path).astype(jnp.int32)
    pl.semaphore_wait(barrier, beside + n_lr - 1)

    def tell():
        neighbours(lambda there, way: pl.semaphore_signal(
            told.at[way], inc=1, device_id={"path": there}, device_id_type=MESH
        ))

    def hear():
        @pl.when(z >= 1)
        def _():
            pl.semaphore_wait(told.at[0], 1)
        @pl.when(z + 1 < n_path)
        def _():
            pl.semaphore_wait(told.at[1], 1)

    if n_path > 2:
        tell()

    def remote(src, dst, send, recv, device):
        return pltpu.make_async_remote_copy(
            src_ref=src, dst_ref=dst, send_sem=send, recv_sem=recv, device_id=device, device_id_type=MESH
        )

    prefix_copies = []
    for k in range(1, n_path):
        prefix_copies.append(remote(
            left_prefix, left_rows.at[z], pre_send.at[k - 1], pre_recv.at[k - 1],
            {"path": lax.rem(z + k, n_path)},
        ))
    for k in range(1, n_lr):
        there = lax.rem(mine + k, n_lr)
        slot = n_path - 1 + k - 1
        prefix_copies.append(remote(
            right_prefix, right_rows.at[z, mine], pre_send.at[slot], pre_recv.at[slot],
            {"half": there // n_tile, "tile": lax.rem(there, n_tile)},
        ))
    for copy in prefix_copies[n_path - 1:]:
        copy.start()

    def rows_l(block, core, i):
        return pl.ds(
            pl.multiple_of((block * n_tile + core) * block_l + i * chunk_l, chunk_l), chunk_l
        )

    def left_flush(block, core, i):
        span = rows_l(block, core, i)
        at = (block * n_tile + core) * count_l + i
        return pltpu.make_async_copy(left_st.at[span], left_out.at[span], lo_sem.at[at])

    def part(block, core):
        return pl.ds(pl.multiple_of(block * block_r + core * part_r, part_r), part_r)

    def right_flush(block, core):
        span = part(block, core)
        return pltpu.make_async_copy(
            right_st.at[span], right_out.at[span], ro_sem.at[block * n_tile + core]
        )

    class Line:
        def __init__(self, axis, pos, n, rows, buf, first, proj, count, sems):
            self.axis, self.pos, self.n, self.rows, self.buf = axis, pos, n, rows, buf
            self.first, self.proj, self.count = first, proj, count
            self.send, self.recv, self.sib_send, self.sib_recv = sems
            self.slots = (n - 1) * count

        def block(self, way, d):
            return self.pos - d if way == 0 else self.pos + d

        def has(self, way, d):
            return (self.pos >= d) if way == 0 else (self.pos + d < self.n)

        def sends(self, way, d):
            onward = (self.pos + 1 < self.n) if way == 0 else (self.pos >= 1)
            return jnp.logical_and(self.has(way, d), onward)

        def onward(self, way, d, i, own=False):
            span = self.rows(self.block(way, d), c, i)
            src = self.first(i) if own else self.buf.at[span]
            at = d * self.count + i
            return remote(
                src, self.buf.at[span], self.send.at[way, at], self.recv.at[way, at],
                {self.axis: self.pos + (1 if way == 0 else -1)},
            )

        def arrived(self, way, d, i):
            span = self.rows(self.block(way, d), c, i)
            at = (d - 1) * self.count + i
            return remote(
                self.buf.at[span], self.buf.at[span], self.send.at[way, at], self.recv.at[way, at],
                {self.axis: self.pos + (1 if way == 0 else -1)},
            )

        def share(self, way, d, i, core):
            span = self.rows(self.block(way, d), core, i)
            at = (d - 1) * self.count + i
            return remote(
                self.buf.at[span], self.buf.at[span],
                self.sib_send.at[way, at], self.sib_recv.at[way, at], {"tile": sib},
            )

        def start_own(self, i):
            for way in (0, 1):
                @pl.when(self.sends(way, 0))
                def _():
                    self.onward(way, 0, i, own=True).start()

        def relay(self, s):
            d, i = s // self.count + 1, lax.rem(s, self.count)
            for way in (0, 1):
                @pl.when(jnp.logical_and(s < self.slots, self.has(way, d)))
                def _():
                    self.arrived(way, d, i).wait_recv()
                    @pl.when(jnp.logical_and(self.sends(way, d), d < self.n - 1))
                    def _():
                        self.onward(way, d, i).start()
                    self.share(way, d, i, c).start()

        def multiply(self, block, core, i):
            span = self.rows(block, core, i)
            left_st[span, :] = lax.dot_general(
                self.buf[span, :], self.proj[...], NT, preferred_element_type=jnp.float32
            ).astype(jnp.bfloat16)
            left_flush(block, core, i).start()

        def compute(self, s):
            d, i = s // self.count + 1, lax.rem(s, self.count)
            for way in (0, 1):
                @pl.when(jnp.logical_and(s < self.slots, self.has(way, d)))
                def _():
                    self.multiply(self.block(way, d), c, i)

        def compute_shared(self, s):
            d, i = s // self.count + 1, lax.rem(s, self.count)
            for way in (0, 1):
                @pl.when(jnp.logical_and(jnp.logical_and(s >= 0, s < self.slots), self.has(way, d)))
                def _():
                    self.share(way, d, i, sib).wait_recv()
                    self.multiply(self.block(way, d), sib, i)

        def finish(self, s):
            d, i = s // self.count, lax.rem(s, self.count)
            for way in (0, 1):
                @pl.when(self.sends(way, d))
                def _():
                    self.onward(way, d, i).wait_send()
                @pl.when(self.has(way, d + 1))
                def _():
                    self.share(way, d + 1, i, c).wait_send()

    left = Line(
        "half", x, n_half, rows_l, left_w,
        lambda i: left_layer.at[pl.ds(i * chunk_l, chunk_l)],
        left_proj, count_l, (l_send, l_recv, l_sib_send, l_sib_recv),
    )

    def own_share(i, core):
        span = rows_l(x, core, i)
        return remote(
            left.first(i), left_w.at[span], o_send.at[i], o_recv.at[i], {"tile": sib}
        )

    for i in range(count_l):
        left.start_own(i)
    for i in range(count_l):
        own_share(i, c).start()

    hot_l[...] = one_hot(hot_l.shape[1], left_map[...])
    hot_r[...] = one_hot(hot_r.shape[1], right_map[...])
    if n_path > 2:
        hear()
        for _ in range(n_path - 3):
            tell()
            hear()
    def prefix_half(block, core):
        return right_rows.at[block, pl.ds(core * half_lr, half_lr)]

    def prefix_out(to):
        held = prefix_half(z, c)
        return remote(held, held, pz_send.at[to], pz_recv.at[z], {"path": to})

    def prefix_in(block):
        held = prefix_half(block, c)
        return remote(held, held, pz_send.at[block], pz_recv.at[block], {"path": block})

    def prefix_share(block, core):
        held = prefix_half(block, core)
        return remote(held, held, ps_send.at[block], ps_recv.at[block], {"tile": sib})

    def state_out(to):
        return remote(
            stage.at[to], right_st.at[part(z, c)], st_send.at[to], st_recv.at[z], {"path": to}
        )

    def state_in(block):
        return remote(
            stage.at[block], right_st.at[part(block, c)], st_send.at[block], st_recv.at[block],
            {"path": block},
        )

    def state_share(block, core):
        held = right_st.at[part(block, core)]
        return remote(held, held, ss_send.at[block], ss_recv.at[block], {"tile": sib})

    def each(d, do):
        @pl.when(z >= d)
        def _():
            do(z - d)
        @pl.when(z + d < n_path)
        def _():
            do(z + d)

    own[1].wait()
    for copy in prefix_copies[n_path - 1:]:
        copy.wait_recv()
    def far_first(k, _):
        each(n_path - 1 - k, lambda to: prefix_out(to).start())
        return 0
    if n_path > 1:
        lax.fori_loop(0, n_path - 1, far_first, 0)

    for copy in prefix_copies[:n_path - 1]:
        copy.start()

    def project_right(block):
        chosen = picked_rows(hot_r[...], right_rows[block])
        right_proj[...] = (chosen * right_factor[...].astype(jnp.float32)).astype(jnp.bfloat16)

    def right_times(rows):
        return lax.dot_general(
            rows, right_proj[...], NT, preferred_element_type=jnp.float32
        ).astype(jnp.bfloat16)

    def right_step(d):
        def pass_on(block):
            prefix_in(block).wait_recv()
            prefix_share(block, c).start()
        each(d, pass_on)

        def form(block):
            prefix_share(block, sib).wait_recv()
            project_right(block)
            stage[block] = right_times(right_w[pl.ds(pl.multiple_of(c * part_r, part_r), part_r), :])
            state_out(block).start()
        each(d, form)

    def left_step(s):
        left.relay(s)
        left.compute_shared(s - 1)
        left.compute(s)

    own[3].wait()
    project_right(z)
    for core in range(n_tile):
        right_st[part(z, core), :] = right_times(right_w[core * part_r:(core + 1) * part_r, :])
        right_flush(z, core).start()
    if n_path > 1:
        lax.fori_loop(0, n_path - 1, lambda t, _: (right_step(t + 1), 0)[1], 0)

    own[0].wait()
    for copy in prefix_copies[:n_path - 1]:
        copy.wait_recv()
    chosen = picked_rows(hot_l[...], left_rows[...])
    left_proj[...] = (chosen * left_proj[...].astype(jnp.float32)).astype(jnp.bfloat16)
    own[2].wait()
    for i in range(count_l):
        left.multiply(x, c, i)
    for i in range(count_l):
        own_share(i, sib).wait_recv()
        left.multiply(x, sib, i)
    if left.slots > 0:
        lax.fori_loop(0, left.slots, lambda t, _: (left_step(t), 0)[1], 0)

    def take(k, _):
        def landed(block):
            state_in(block).wait_recv()
            state_share(block, c).start()
            right_flush(block, c).start()
        each(k + 1, landed)
        return 0

    if n_path > 1:
        lax.fori_loop(0, n_path - 1, take, 0)
    def take_shared(k, _):
        def landed(block):
            state_share(block, sib).wait_recv()
            right_flush(block, sib).start()
        each(k + 1, landed)
        return 0

    if n_path > 1:
        lax.fori_loop(0, n_path - 1, take_shared, 0)
    left.compute_shared(jnp.int32(left.slots - 1))

    def close(k, _):
        def ended(block):
            prefix_out(block).wait_send()
            prefix_share(block, c).wait_send()
            state_out(block).wait_send()
            state_share(block, c).wait_send()
        each(k + 1, ended)
        return 0

    if n_path > 1:
        lax.fori_loop(0, n_path - 1, close, 0)
    if left.slots > 0:
        lax.fori_loop(0, left.slots, lambda s, _: (left.finish(s), 0)[1], 0)
    for i in range(count_l):
        own_share(i, c).wait_send()
    for copy in prefix_copies:
        copy.wait_send()

    def flushed_left(k, _):
        for core in range(n_tile):
            for i in range(count_l):
                left_flush(k, core, i).wait()
        return 0

    def flushed_right(k, _):
        for core in range(n_tile):
            right_flush(k, core).wait()
        return 0

    lax.fori_loop(0, n_half, flushed_left, 0)
    lax.fori_loop(0, n_path, flushed_right, 0)


def on_device(
    sizes,
    left_prefix, right_prefix, left_layer, right_layer, left_map, right_map, branch_bits, cut_side,
):
    n_half, n_path, n_tile = sizes
    n_lr = n_half * n_tile
    paths = left_map.shape[0]
    gate = left_layer.shape[1]
    hi_l, hi_r = left_layer.shape[0] * n_lr, right_layer.shape[0] * n_path
    part_r = right_layer.shape[0] // n_tile
    count_l = left_layer.shape[0] // max(16, left_layer.shape[0] // 4)
    slots_l = max(1, (n_half - 1) * count_l)
    pre = n_path + n_lr - 2
    dma = pltpu.SemaphoreType.DMA
    vmem = pl.BlockSpec(memory_space=pltpu.VMEM)
    anywhere = pl.BlockSpec(memory_space=pl.ANY)
    left_states, right_states = pl.pallas_call(
        functools.partial(kernel, sizes),
        out_shape=(
            jax.ShapeDtypeStruct((hi_l, paths), jnp.bfloat16),
            jax.ShapeDtypeStruct((hi_r, paths), jnp.bfloat16),
        ),
        in_specs=[anywhere] * 4 + [vmem] * 4,
        out_specs=(anywhere, anywhere),
        scratch_shapes=[
            pltpu.VMEM((n_path,) + left_prefix.shape, jnp.bfloat16),
            pltpu.VMEM((n_path, n_lr) + right_prefix.shape, jnp.bfloat16),
            pltpu.VMEM((paths, gate), jnp.bfloat16),
            pltpu.VMEM((paths, gate), jnp.bfloat16),
            pltpu.VMEM((paths, gate), jnp.bfloat16),
            pltpu.VMEM((hi_l, gate), jnp.bfloat16),
            pltpu.VMEM(right_layer.shape, jnp.bfloat16),
            pltpu.VMEM((hi_l, paths), jnp.bfloat16),
            pltpu.VMEM((hi_r, paths), jnp.bfloat16),
            pltpu.VMEM((n_path, part_r, paths), jnp.bfloat16),
            pltpu.VMEM((paths, left_prefix.shape[0] * n_path), jnp.bfloat16),
            pltpu.VMEM((paths, right_prefix.shape[0] * n_lr), jnp.bfloat16),
            pltpu.SemaphoreType.REGULAR((2,)),
            dma((4,)), dma((pre,)), dma((pre,)),
        ] + [dma((n_path,))] * 8 + [
            dma((2, slots_l)), dma((2, slots_l)), dma((2, slots_l)), dma((2, slots_l)),
            dma((count_l,)), dma((count_l,)),
            dma((n_lr * count_l,)), dma((n_path * n_tile,)),
        ],
        compiler_params=pltpu.CompilerParams(collective_id=0, has_side_effects=True),
    )(
        left_prefix, right_prefix, left_layer, right_layer,
        left_map[None, :], right_map[None, :], branch_bits.T, cut_side[None, :],
    )
    amplitude = lax.dot_general(
        left_states, right_states, NT, preferred_element_type=jnp.float32
    )
    return amplitude.astype(jnp.bfloat16)


def solution(mesh):
    in_specs = (
        P(("groups", "path"), ("half", "tile")),
        P(("groups", "half", "tile"), "path"),
        P(("groups", "half", "tile"), None),
        P(("groups", "path"), None),
        P("groups"),
        P("groups"),
        P("groups", None),
        P("groups"),
    )
    out_specs = P(("groups", "half", "tile"), "path")
    sizes = tuple(mesh.shape[axis] for axis in ("half", "path", "tile"))
    return jax.shard_map(
        functools.partial(on_device, sizes),
        mesh=mesh, in_specs=in_specs, out_specs=out_specs, check_vma=False,
    )
```

```python
import functools

import jax
import jax.numpy as jnp
from jax import lax
from jax.experimental import pallas as pl
from jax.experimental.pallas import tpu as pltpu
from jax.sharding import PartitionSpec as P

MESH = pl.DeviceIdType.MESH
NT = (((1,), (1,)), ((), ()))
TN = (((0,), (0,)), ((), ()))


def factors(branch, side_row, gate_count):
    cuts = branch.shape[0]
    across = lax.broadcasted_iota(jnp.int32, (cuts, cuts), 0)
    down = lax.broadcasted_iota(jnp.int32, (cuts, cuts), 1)
    side = jnp.sum(jnp.where(across == down, side_row, 0.0), axis=1, keepdims=True)
    place = lax.broadcasted_iota(jnp.int32, (cuts, gate_count), 0)
    code = lax.broadcasted_iota(jnp.int32, (cuts, gate_count), 1)
    bits = (jnp.right_shift(code, place) & 1).astype(jnp.float32)

    def dot(columns, table):
        return lax.dot_general(
            columns.astype(jnp.bfloat16), table.astype(jnp.bfloat16), TN,
            preferred_element_type=jnp.float32,
        )

    made = []
    for projector in (side, 1.0 - side):
        chosen = branch * projector
        misses = dot(chosen, 1.0 - bits) + dot(projector - chosen, bits)
        parity = dot(branch - chosen, bits).astype(jnp.int32) & 1
        sign = (1 - 2 * parity).astype(jnp.float32)
        made.append(jnp.where(misses == 0.0, sign, 0.0))
    return made


def one_hot(rows, path_map):
    which = lax.broadcasted_iota(jnp.int32, (rows, path_map.shape[1]), 0)
    return jnp.where(which == path_map, 1.0, 0.0).T.astype(jnp.bfloat16)


def picked_rows(hot, prefix):
    gate_count = prefix.shape[-1]
    rows = prefix.astype(jnp.float32).reshape(-1, gate_count).astype(jnp.bfloat16)
    return jnp.dot(hot, rows, preferred_element_type=jnp.float32)


def kernel(
    sizes,
    left_prefix, right_prefix, left_layer, right_layer, left_map, right_map, branch_bits, cut_side,
    left_out, right_out,
    left_rows, right_rows, left_proj, right_factor, right_proj, left_w, right_w,
    left_st, right_st, stage, hot_l, hot_r, told,
    own_sem, pre_send, pre_recv,
    pz_send, pz_recv, ps_send, ps_recv,
    st_send, st_recv, ss_send, ss_recv,
    l_send, l_recv, l_sib_send, l_sib_recv, o_send, o_recv, lo_sem, ro_sem,
):
    n_half, n_path, n_tile = sizes
    x, z, c = lax.axis_index("half"), lax.axis_index("path"), lax.axis_index("tile")
    sib = 1 - c
    n_lr = n_half * n_tile
    mine = x * n_tile + c

    barrier = pltpu.get_barrier_semaphore()
    def neighbours(do):
        @pl.when(z >= 1)
        def _():
            do(z - 1, 1)
        @pl.when(z + 1 < n_path)
        def _():
            do(z + 1, 0)

    neighbours(lambda there, _: pl.semaphore_signal(
        barrier, inc=1, device_id={"path": there}, device_id_type=MESH
    ))
    for k in range(1, n_lr):
        there = lax.rem(mine + k, n_lr)
        pl.semaphore_signal(
            barrier,
            inc=1,
            device_id={"half": there // n_tile, "tile": lax.rem(there, n_tile)},
            device_id_type=MESH,
        )

    block_l, gate = left_layer.shape
    block_r = right_layer.shape[0]
    part_r = block_r // n_tile
    chunk_l = max(16, block_l // 4)
    count_l = block_l // chunk_l
    half_lr = n_lr // n_tile

    own = [
        pltpu.make_async_copy(left_prefix, left_rows.at[z], own_sem.at[0]),
        pltpu.make_async_copy(right_prefix, right_rows.at[z, mine], own_sem.at[1]),
        pltpu.make_async_copy(
            left_layer, left_w.at[pl.ds(pl.multiple_of(mine * block_l, block_l), block_l)], own_sem.at[2]
        ),
        pltpu.make_async_copy(right_layer, right_w, own_sem.at[3]),
    ]
    for copy in own:
        copy.start()

    side = cut_side[...].astype(jnp.float32)
    branch = branch_bits[...].astype(jnp.float32)
    for ref, factor in zip((left_proj, right_factor), factors(branch, side, gate)):
        ref[...] = factor.astype(jnp.bfloat16)

    beside = (z >= 1).astype(jnp.int32) + (z + 1 < n_path).astype(jnp.int32)
    pl.semaphore_wait(barrier, beside + n_lr - 1)

    def tell():
        neighbours(lambda there, way: pl.semaphore_signal(
            told.at[way], inc=1, device_id={"path": there}, device_id_type=MESH
        ))

    def hear():
        @pl.when(z >= 1)
        def _():
            pl.semaphore_wait(told.at[0], 1)
        @pl.when(z + 1 < n_path)
        def _():
            pl.semaphore_wait(told.at[1], 1)

    if n_path > 2:
        tell()

    def remote(src, dst, send, recv, device):
        return pltpu.make_async_remote_copy(
            src_ref=src, dst_ref=dst, send_sem=send, recv_sem=recv, device_id=device, device_id_type=MESH
        )

    prefix_copies = []
    for k in range(1, n_path):
        prefix_copies.append(remote(
            left_prefix, left_rows.at[z], pre_send.at[k - 1], pre_recv.at[k - 1],
            {"path": lax.rem(z + k, n_path)},
        ))
    for k in range(1, n_lr):
        there = lax.rem(mine + k, n_lr)
        slot = n_path - 1 + k - 1
        prefix_copies.append(remote(
            right_prefix, right_rows.at[z, mine], pre_send.at[slot], pre_recv.at[slot],
            {"half": there // n_tile, "tile": lax.rem(there, n_tile)},
        ))
    for copy in prefix_copies[n_path - 1:]:
        copy.start()

    def rows_l(block, core, i):
        return pl.ds(
            pl.multiple_of((block * n_tile + core) * block_l + i * chunk_l, chunk_l), chunk_l
        )

    def left_flush(block, core, i):
        span = rows_l(block, core, i)
        at = (block * n_tile + core) * count_l + i
        return pltpu.make_async_copy(left_st.at[span], left_out.at[span], lo_sem.at[at])

    def part(block, core):
        return pl.ds(pl.multiple_of(block * block_r + core * part_r, part_r), part_r)

    def right_flush(block, core):
        span = part(block, core)
        return pltpu.make_async_copy(
            right_st.at[span], right_out.at[span], ro_sem.at[block * n_tile + core]
        )

    class Line:
        def __init__(self, axis, pos, n, rows, buf, first, proj, count, sems):
            self.axis, self.pos, self.n, self.rows, self.buf = axis, pos, n, rows, buf
            self.first, self.proj, self.count = first, proj, count
            self.send, self.recv, self.sib_send, self.sib_recv = sems
            self.slots = (n - 1) * count

        def block(self, way, d):
            return self.pos - d if way == 0 else self.pos + d

        def has(self, way, d):
            return (self.pos >= d) if way == 0 else (self.pos + d < self.n)

        def sends(self, way, d):
            onward = (self.pos + 1 < self.n) if way == 0 else (self.pos >= 1)
            return jnp.logical_and(self.has(way, d), onward)

        def onward(self, way, d, i, own=False):
            span = self.rows(self.block(way, d), c, i)
            src = self.first(i) if own else self.buf.at[span]
            at = d * self.count + i
            return remote(
                src, self.buf.at[span], self.send.at[way, at], self.recv.at[way, at],
                {self.axis: self.pos + (1 if way == 0 else -1)},
            )

        def arrived(self, way, d, i):
            span = self.rows(self.block(way, d), c, i)
            at = (d - 1) * self.count + i
            return remote(
                self.buf.at[span], self.buf.at[span], self.send.at[way, at], self.recv.at[way, at],
                {self.axis: self.pos + (1 if way == 0 else -1)},
            )

        def share(self, way, d, i, core):
            span = self.rows(self.block(way, d), core, i)
            at = (d - 1) * self.count + i
            return remote(
                self.buf.at[span], self.buf.at[span],
                self.sib_send.at[way, at], self.sib_recv.at[way, at], {"tile": sib},
            )

        def start_own(self, i):
            for way in (0, 1):
                @pl.when(self.sends(way, 0))
                def _():
                    self.onward(way, 0, i, own=True).start()

        def relay(self, s):
            d, i = s // self.count + 1, lax.rem(s, self.count)
            for way in (0, 1):
                @pl.when(jnp.logical_and(s < self.slots, self.has(way, d)))
                def _():
                    self.arrived(way, d, i).wait_recv()
                    @pl.when(jnp.logical_and(self.sends(way, d), d < self.n - 1))
                    def _():
                        self.onward(way, d, i).start()
                    self.share(way, d, i, c).start()

        def multiply(self, block, core, i):
            span = self.rows(block, core, i)
            left_st[span, :] = lax.dot_general(
                self.buf[span, :], self.proj[...], NT, preferred_element_type=jnp.float32
            ).astype(jnp.bfloat16)
            left_flush(block, core, i).start()

        def compute(self, s):
            d, i = s // self.count + 1, lax.rem(s, self.count)
            for way in (0, 1):
                @pl.when(jnp.logical_and(s < self.slots, self.has(way, d)))
                def _():
                    self.multiply(self.block(way, d), c, i)

        def compute_shared(self, s):
            d, i = s // self.count + 1, lax.rem(s, self.count)
            for way in (0, 1):
                @pl.when(jnp.logical_and(jnp.logical_and(s >= 0, s < self.slots), self.has(way, d)))
                def _():
                    self.share(way, d, i, sib).wait_recv()
                    self.multiply(self.block(way, d), sib, i)

        def finish(self, s):
            d, i = s // self.count, lax.rem(s, self.count)
            for way in (0, 1):
                @pl.when(self.sends(way, d))
                def _():
                    self.onward(way, d, i).wait_send()
                @pl.when(self.has(way, d + 1))
                def _():
                    self.share(way, d + 1, i, c).wait_send()

    left = Line(
        "half", x, n_half, rows_l, left_w,
        lambda i: left_layer.at[pl.ds(i * chunk_l, chunk_l)],
        left_proj, count_l, (l_send, l_recv, l_sib_send, l_sib_recv),
    )

    def own_share(i, core):
        span = rows_l(x, core, i)
        return remote(
            left.first(i), left_w.at[span], o_send.at[i], o_recv.at[i], {"tile": sib}
        )

    for i in range(count_l):
        left.start_own(i)
    for i in range(count_l):
        own_share(i, c).start()

    hot_l[...] = one_hot(hot_l.shape[1], left_map[...])
    hot_r[...] = one_hot(hot_r.shape[1], right_map[...])
    if n_path > 2:
        hear()
        for _ in range(n_path - 3):
            tell()
            hear()
    def prefix_half(block, core):
        return right_rows.at[block, pl.ds(core * half_lr, half_lr)]

    def prefix_out(to):
        held = prefix_half(z, c)
        return remote(held, held, pz_send.at[to], pz_recv.at[z], {"path": to})

    def prefix_in(block):
        held = prefix_half(block, c)
        return remote(held, held, pz_send.at[block], pz_recv.at[block], {"path": block})

    def prefix_share(block, core):
        held = prefix_half(block, core)
        return remote(held, held, ps_send.at[block], ps_recv.at[block], {"tile": sib})

    def state_out(to):
        return remote(
            stage.at[to], right_st.at[part(z, c)], st_send.at[to], st_recv.at[z], {"path": to}
        )

    def state_in(block):
        return remote(
            stage.at[block], right_st.at[part(block, c)], st_send.at[block], st_recv.at[block],
            {"path": block},
        )

    def state_share(block, core):
        held = right_st.at[part(block, core)]
        return remote(held, held, ss_send.at[block], ss_recv.at[block], {"tile": sib})

    def each(d, do):
        @pl.when(z >= d)
        def _():
            do(z - d)
        @pl.when(z + d < n_path)
        def _():
            do(z + d)

    own[1].wait()
    for copy in prefix_copies[n_path - 1:]:
        copy.wait_recv()
    def far_first(k, _):
        each(n_path - 1 - k, lambda to: prefix_out(to).start())
        return 0
    if n_path > 1:
        lax.fori_loop(0, n_path - 1, far_first, 0)

    for copy in prefix_copies[:n_path - 1]:
        copy.start()

    def project_right(block):
        chosen = picked_rows(hot_r[...], right_rows[block])
        right_proj[...] = (chosen * right_factor[...].astype(jnp.float32)).astype(jnp.bfloat16)

    def right_times(rows):
        return lax.dot_general(
            rows, right_proj[...], NT, preferred_element_type=jnp.float32
        ).astype(jnp.bfloat16)

    def right_step(d):
        def pass_on(block):
            prefix_in(block).wait_recv()
            prefix_share(block, c).start()
        each(d, pass_on)

    def right_form(d):
        def form(block):
            prefix_share(block, sib).wait_recv()
            project_right(block)
            stage[block] = right_times(right_w[pl.ds(pl.multiple_of(c * part_r, part_r), part_r), :])
            state_out(block).start()
        each(d, form)

    def left_step(s):
        left.relay(s)
        left.compute_shared(s - 1)
        left.compute(s)

    own[3].wait()
    project_right(z)
    for core in range(n_tile):
        right_st[part(z, core), :] = right_times(right_w[core * part_r:(core + 1) * part_r, :])
        right_flush(z, core).start()
    if n_path > 1:
        lax.fori_loop(0, n_path - 1, lambda t, _: (right_step(t + 1), 0)[1], 0)
        lax.fori_loop(0, n_path - 1, lambda t, _: (right_form(t + 1), 0)[1], 0)

    own[0].wait()
    for copy in prefix_copies[:n_path - 1]:
        copy.wait_recv()
    chosen = picked_rows(hot_l[...], left_rows[...])
    left_proj[...] = (chosen * left_proj[...].astype(jnp.float32)).astype(jnp.bfloat16)
    own[2].wait()
    for i in range(count_l):
        left.multiply(x, c, i)
    for i in range(count_l):
        own_share(i, sib).wait_recv()
        left.multiply(x, sib, i)
    if left.slots > 0:
        lax.fori_loop(0, left.slots, lambda t, _: (left_step(t), 0)[1], 0)

    def take(k, _):
        def landed(block):
            state_in(block).wait_recv()
            state_share(block, c).start()
            right_flush(block, c).start()
        each(k + 1, landed)
        return 0

    if n_path > 1:
        lax.fori_loop(0, n_path - 1, take, 0)
    def take_shared(k, _):
        def landed(block):
            state_share(block, sib).wait_recv()
            right_flush(block, sib).start()
        each(k + 1, landed)
        return 0

    if n_path > 1:
        lax.fori_loop(0, n_path - 1, take_shared, 0)
    left.compute_shared(jnp.int32(left.slots - 1))

    def close(k, _):
        def ended(block):
            prefix_out(block).wait_send()
            prefix_share(block, c).wait_send()
            state_out(block).wait_send()
            state_share(block, c).wait_send()
        each(k + 1, ended)
        return 0

    if n_path > 1:
        lax.fori_loop(0, n_path - 1, close, 0)
    if left.slots > 0:
        lax.fori_loop(0, left.slots, lambda s, _: (left.finish(s), 0)[1], 0)
    for i in range(count_l):
        own_share(i, c).wait_send()
    for copy in prefix_copies:
        copy.wait_send()

    def flushed_left(k, _):
        for core in range(n_tile):
            for i in range(count_l):
                left_flush(k, core, i).wait()
        return 0

    def flushed_right(k, _):
        for core in range(n_tile):
            right_flush(k, core).wait()
        return 0

    lax.fori_loop(0, n_half, flushed_left, 0)
    lax.fori_loop(0, n_path, flushed_right, 0)


def on_device(
    sizes,
    left_prefix, right_prefix, left_layer, right_layer, left_map, right_map, branch_bits, cut_side,
):
    n_half, n_path, n_tile = sizes
    n_lr = n_half * n_tile
    paths = left_map.shape[0]
    gate = left_layer.shape[1]
    hi_l, hi_r = left_layer.shape[0] * n_lr, right_layer.shape[0] * n_path
    part_r = right_layer.shape[0] // n_tile
    count_l = left_layer.shape[0] // max(16, left_layer.shape[0] // 4)
    slots_l = max(1, (n_half - 1) * count_l)
    pre = n_path + n_lr - 2
    dma = pltpu.SemaphoreType.DMA
    vmem = pl.BlockSpec(memory_space=pltpu.VMEM)
    anywhere = pl.BlockSpec(memory_space=pl.ANY)
    left_states, right_states = pl.pallas_call(
        functools.partial(kernel, sizes),
        out_shape=(
            jax.ShapeDtypeStruct((hi_l, paths), jnp.bfloat16),
            jax.ShapeDtypeStruct((hi_r, paths), jnp.bfloat16),
        ),
        in_specs=[anywhere] * 4 + [vmem] * 4,
        out_specs=(anywhere, anywhere),
        scratch_shapes=[
            pltpu.VMEM((n_path,) + left_prefix.shape, jnp.bfloat16),
            pltpu.VMEM((n_path, n_lr) + right_prefix.shape, jnp.bfloat16),
            pltpu.VMEM((paths, gate), jnp.bfloat16),
            pltpu.VMEM((paths, gate), jnp.bfloat16),
            pltpu.VMEM((paths, gate), jnp.bfloat16),
            pltpu.VMEM((hi_l, gate), jnp.bfloat16),
            pltpu.VMEM(right_layer.shape, jnp.bfloat16),
            pltpu.VMEM((hi_l, paths), jnp.bfloat16),
            pltpu.VMEM((hi_r, paths), jnp.bfloat16),
            pltpu.VMEM((n_path, part_r, paths), jnp.bfloat16),
            pltpu.VMEM((paths, left_prefix.shape[0] * n_path), jnp.bfloat16),
            pltpu.VMEM((paths, right_prefix.shape[0] * n_lr), jnp.bfloat16),
            pltpu.SemaphoreType.REGULAR((2,)),
            dma((4,)), dma((pre,)), dma((pre,)),
        ] + [dma((n_path,))] * 8 + [
            dma((2, slots_l)), dma((2, slots_l)), dma((2, slots_l)), dma((2, slots_l)),
            dma((count_l,)), dma((count_l,)),
            dma((n_lr * count_l,)), dma((n_path * n_tile,)),
        ],
        compiler_params=pltpu.CompilerParams(collective_id=0, has_side_effects=True),
    )(
        left_prefix, right_prefix, left_layer, right_layer,
        left_map[None, :], right_map[None, :], branch_bits.T, cut_side[None, :],
    )
    amplitude = lax.dot_general(
        left_states, right_states, NT, preferred_element_type=jnp.float32
    )
    return amplitude.astype(jnp.bfloat16)


def solution(mesh):
    in_specs = (
        P(("groups", "path"), ("half", "tile")),
        P(("groups", "half", "tile"), "path"),
        P(("groups", "half", "tile"), None),
        P(("groups", "path"), None),
        P("groups"),
        P("groups"),
        P("groups", None),
        P("groups"),
    )
    out_specs = P(("groups", "half", "tile"), "path")
    sizes = tuple(mesh.shape[axis] for axis in ("half", "path", "tile"))
    return jax.shard_map(
        functools.partial(on_device, sizes),
        mesh=mesh, in_specs=in_specs, out_specs=out_specs, check_vma=False,
    )
```
